32 devices in a mesh: section: 4 (over y, x), fsdp: 8 (over z, core).
Axes of the slice: x: 2, y: 2, z: 4, core: 2. Of those that a mesh axis runs over, the one named last changes fastest.
Arguments:
- enc_states: bfloat16 [8, 4, 1280], P('fsdp'), may hold values from -6 to 6
- clip_frames: int32 [8], replicated, may hold values from 2 to 4, as said below
- clip_offset: int32 [8], replicated, may hold values from 0 to 126, as said below
- ln_gain: float32 [1280], replicated, may hold values from 0.1 to 1.9
- ln_bias: float32 [1280], replicated, may hold values from -0.6 to 0.6
- w_proj: bfloat16 [1280, 8192], P(None, 'fsdp'), may hold values from -0.15625 to 0.15625
- proj_bias: float32 [8192], P('fsdp'), may hold values from -3 to 3
- text_embed: bfloat16 [64, 2, 8192], P(None, None, 'fsdp'), may hold values from -6 to 6
- norm_gain: float32 [4, 8192], P('section'), may hold values from 0.1 to 1.9
- w_gate: bfloat16 [4, 14784, 8192], P('section', 'fsdp'), may hold values from -0.0625 to 0.0625
- w_up: bfloat16 [4, 14784, 8192], P('section', 'fsdp'), may hold values from -0.0625 to 0.0625
- w_down: bfloat16 [4, 14784, 8192], P('section', 'fsdp'), may hold values from -0.046875 to 0.046875
Outputs:
- stream_out: bfloat16 [64, 2, 8192], P('section', None, 'fsdp')
The draws below stay inside these ranges and needn't reach their ends.
Inputs may be any that keep to these rules, and one draw needn't show every extreme that they name: `clip_frames`: every clip's frame count is even, and some clip has exactly 4 frames. Clip c's live rows occupy stream positions clip_offset[c] to clip_offset[c] + clip_frames[c] / 2 - 1, all inside one microbatch (positions m * 64 to (m + 1) * 64 - 1); no two clips share a position; each microbatch holds 4 clips.
All inputs are finite; a program needn't handle non-finite values.
Results may differ from the reference program's by a relative error of at most 0.015.
Values may be sent and summed in bfloat16 or wider, within the bound.
No kernel may reach another device: no remote copies, remote signals or barrier semaphores. Data moves between devices by JAX's collectives and lax.ppermute only.
A program may use at most 192 MiB of HBM per device.

```python
import jax
import jax.numpy as jnp
from jax import lax

D = 8192
FF = 14784
DE = 1280
CLIP_ROWS = 2
MICRO = 2
TOKENS = 64
FRAMES = 4
CLIPS = 8
LAYERS = 4


def clip_layout(key):
    base = jax.random.fold_in(key, 11)
    key_rows, key_order, key_gaps = jax.random.split(base, 3)
    counts = jax.random.randint(key_rows, (CLIPS,), 1, CLIP_ROWS + 1).astype(jnp.int32)
    counts = counts.at[0].set(CLIP_ROWS)
    rest = (jax.random.permutation(key_order, CLIPS - 1) + 1).astype(jnp.int32)
    order = jnp.concatenate([rest, jnp.zeros((1,), jnp.int32)]).astype(jnp.int32)
    per_micro = CLIPS // MICRO
    slot_rows = counts[order].reshape(MICRO, per_micro)
    spare = TOKENS - jnp.sum(slot_rows, axis=1)
    weights = jax.random.randint(key_gaps, (MICRO, per_micro + 1), 1, 101).astype(jnp.int32)
    gaps = spare[:, None] * weights // jnp.sum(weights, axis=1, keepdims=True)
    gaps = gaps.at[0, 0].set(0)
    before = jnp.cumsum(slot_rows, axis=1) - slot_rows
    starts = jnp.cumsum(gaps[:, :per_micro], axis=1) + before
    starts = starts.at[MICRO - 1, per_micro - 1].set(TOKENS - CLIP_ROWS)
    starts = starts + (jnp.arange(MICRO, dtype=jnp.int32) * TOKENS)[:, None]
    offsets = jnp.zeros((CLIPS,), jnp.int32).at[order].set(starts.reshape(-1).astype(jnp.int32))
    return (2 * counts, offsets)


def draw_clip_frames(key, part):
    frames, offsets = clip_layout(key)
    return frames


def draw_clip_offset(key, part):
    frames, offsets = clip_layout(key)
    return offsets


def level_of(stream_key, shape, shards, smallest, largest):
    loudness = 1.0
    for dim, shards_of in shards:
        heights = jax.random.uniform(jax.random.fold_in(jax.random.fold_in(stream_key, 6), dim), (shards_of,), jnp.float32, smallest / len(shards), largest / len(shards))
        loudness = loudness * jnp.repeat(jnp.exp(heights), shape[dim] // shards_of).reshape((-1,) + (1,) * (len(shape) - 1 - dim))
    return loudness


def scatter_about(rng, shape, deviation, most, cuts=(), kind=jnp.bfloat16):
    result = deviation * jax.random.normal(rng, shape, jnp.float32)
    if cuts:
        result = result * level_of(rng, shape, cuts, -0.22, 0.18)
    return jnp.clip(result, -most, most).astype(kind)


def setup_inputs(seed: int = 0) -> dict:
    key_list = jax.random.split(jax.random.key(seed), 13)
    return {
        "enc_states": scatter_about(key_list[0], (CLIPS, FRAMES, DE), 1.0, 6.0, ((0, 8),)),
        "clip_frames": draw_clip_frames(jax.random.fold_in(key_list[12], 71), 0),
        "clip_offset": draw_clip_offset(jax.random.fold_in(key_list[12], 71), 0),
        "ln_gain": jnp.clip(1.0 + 0.18 * jax.random.normal(key_list[3], (DE,), jnp.float32), 0.1, 1.9),
        "ln_bias": jnp.clip(jax.random.uniform(key_list[4], (DE,), jnp.float32, -0.6, 0.6), -0.6, 0.6),
        "w_proj": scatter_about(key_list[5], (DE, D), DE ** -0.5, 0.15625, ((1, 8),)),
        "proj_bias": scatter_about(key_list[6], (D,), 0.5, 3.0, ((0, 8),), jnp.float32),
        "text_embed": scatter_about(key_list[7], (TOKENS, MICRO, D), 1.0, 6.0, ((2, 8),)),
        "norm_gain": jnp.clip(1.0 + 0.18 * jax.random.normal(key_list[8], (LAYERS, D), jnp.float32), 0.1, 1.9),
        "w_gate": scatter_about(key_list[9], (LAYERS, FF, D), D ** -0.5, 0.0625, ((0, 4), (1, 8))),
        "w_up": scatter_about(key_list[10], (LAYERS, FF, D), D ** -0.5, 0.0625, ((0, 4), (1, 8))),
        "w_down": scatter_about(key_list[11], (LAYERS, FF, D), FF ** -0.5, 0.046875, ((0, 4), (1, 8))),
    }


def rms_scaled(stream, gain):
    values = stream.astype(jnp.float32)
    scale = lax.rsqrt(lax.optimization_barrier(jnp.mean(values * values, axis=-1, keepdims=True)) + 1e-06)
    return (values * scale * gain.astype(jnp.float32)).astype(jnp.bfloat16)

def reference(enc_states, clip_frames, clip_offset, ln_gain, ln_bias, w_proj, proj_bias, text_embed, norm_gain, w_gate, w_up, w_down):
    pairs = enc_states.astype(jnp.float32).reshape(CLIPS, CLIP_ROWS, 2, DE)
    pooled = 0.5 * (pairs[:, :, 0] + pairs[:, :, 1])
    centre = lax.optimization_barrier(jnp.mean(pooled, axis=-1, keepdims=True))
    centred = pooled - centre
    spread = lax.optimization_barrier(jnp.mean(centred * centred, axis=-1, keepdims=True))
    audio_ln = (centred * lax.rsqrt(spread + 1e-05) * ln_gain.astype(jnp.float32) + ln_bias.astype(jnp.float32)).astype(jnp.bfloat16)
    audio_ln = audio_ln.reshape(CLIPS * CLIP_ROWS, DE)
    projected = (jnp.dot(audio_ln, w_proj, preferred_element_type=jnp.float32) + proj_bias.astype(jnp.float32)).astype(jnp.bfloat16)
    within = jnp.arange(CLIP_ROWS, dtype=jnp.int32)
    live = within[None, :] * 2 < clip_frames[:, None]
    spot = clip_offset[:, None] + within[None, :]
    target = jnp.where(live, spot % TOKENS * MICRO + spot // TOKENS, TOKENS * MICRO).astype(jnp.int32).reshape(-1)
    flags = jnp.zeros((TOKENS * MICRO,), jnp.int32).at[target].set(1, mode='drop')
    placed = jnp.zeros((TOKENS * MICRO, D), jnp.bfloat16).at[target].set(projected, mode='drop')
    stream = jnp.where(flags[:, None] == 1, placed, text_embed.reshape(TOKENS * MICRO, D))
    dims = (((1,), (1,)), ((), ()))
    for layer in range(LAYERS):
        normed = rms_scaled(stream, norm_gain[layer])
        gate = lax.dot_general(normed, w_gate[layer], dims, preferred_element_type=jnp.float32)
        up = lax.dot_general(normed, w_up[layer], dims, preferred_element_type=jnp.float32)
        hidden = (jax.nn.silu(gate) * up).astype(jnp.bfloat16)
        branch = jnp.dot(hidden, w_down[layer], preferred_element_type=jnp.float32)
        stream = (stream.astype(jnp.float32) + branch).astype(jnp.bfloat16)
    return stream.reshape(TOKENS, MICRO, D)
```

```python
import jax
import jax.numpy as jnp
from jax import lax
from jax.experimental import pallas as pl
from jax.experimental.pallas import tpu as pltpu
from jax.sharding import PartitionSpec as P


BF = jnp.bfloat16
F32 = jnp.float32
ROWS_BOTH = (((1,), (1,)), ((), ()))
CORES = 2
MOST_CHIPS = 8


def rows_block(total, most):
    best = total
    for size in range(8, min(total, most) + 1, 8):
        if total % size == 0:
            best = size
    return best


def cost(flops, nbytes):
    return pl.CostEstimate(flops=flops, bytes_accessed=nbytes, transcendentals=0)


def sums_of(xg_ref, gate_a, gate_b, up_a, up_b):
    width = gate_a.shape[2]
    xa, xb = xg_ref[:, :width], xg_ref[:, width:]

    def one(wa, wb):
        return lax.dot_general(
            wa[0], xa, ROWS_BOTH, preferred_element_type=F32
        ) + lax.dot_general(wb[0], xb, ROWS_BOTH, preferred_element_type=F32)

    return one(gate_a, gate_b), one(up_a, up_b)


def scaled_rows(xa_ref, xb_ref, gain_a, gain_b, xg_ref):
    width = xa_ref.shape[1]
    parts = 0.0
    for place, (x_ref, gain_ref) in enumerate(((xa_ref, gain_a), (xb_ref, gain_b))):
        values = x_ref[...].astype(F32)
        squares = values * values
        for start in range(0, width, 128):
            parts = parts + squares[:, start : start + 128]
        xg_ref[:, place * width : (place + 1) * width] = (values * gain_ref[...]).astype(BF)
    return parts


def gate_up_call(blocks, xa, xb, gain, gate_w, up_w, carried):
    rows, width = xa.shape
    hidden = gate_w.shape[1]
    size = rows_block(hidden, 264)
    first = carried is None

    def kernel(at, *refs):
        xa_ref, xb_ref, gain_a, gain_b, gate_a, gate_b, up_a, up_b = refs[:8]
        if first:
            gate_out, up_out, parts_out, xg_ref = refs[8:]
        else:
            gate_in, up_in, parts_in, gate_out, up_out, parts_out, xg_ref = refs[8:]

        @pl.when(pl.program_id(0) == 0)
        def _():
            parts = scaled_rows(xa_ref, xb_ref, gain_a, gain_b, xg_ref)
            parts_out[...] = parts if first else parts_in[...] + parts

        gate, up = sums_of(xg_ref, gate_a, gate_b, up_a, up_b)
        if first:
            gate_out[...] = gate
            up_out[...] = up
        else:
            gate_out[...] = gate_in[...] + gate
            up_out[...] = up_in[...] + up

    whole = lambda shape: pl.BlockSpec(shape, lambda i, at: (0,) * len(shape))
    gain_spec = lambda n: pl.BlockSpec((1, width), lambda i, at: (0, at[n]))
    w_spec = lambda n: pl.BlockSpec((1, size, width), lambda i, at: (0, i, at[n]))
    sums = pl.BlockSpec((size, rows), lambda i, at: (i, 0))
    parts_spec = whole((rows, 128))
    in_specs = [whole((rows, width))] * 2 + [gain_spec(0), gain_spec(1)]
    in_specs += [w_spec(0), w_spec(1), w_spec(0), w_spec(1)]
    operands = [xa, xb, gain, gain, gate_w, gate_w, up_w, up_w]
    aliases = {}
    if not first:
        in_specs += [sums, sums, parts_spec]
        operands += list(carried)
        aliases = {9: 0, 10: 1, 11: 2}
    return pl.pallas_call(
        kernel,
        grid_spec=pltpu.PrefetchScalarGridSpec(
            num_scalar_prefetch=1,
            grid=(hidden // size,),
            in_specs=in_specs,
            out_specs=[sums, sums, parts_spec],
            scratch_shapes=[pltpu.VMEM((rows, 2 * width), BF)],
        ),
        out_shape=[
            jax.ShapeDtypeStruct((hidden, rows), F32),
            jax.ShapeDtypeStruct((hidden, rows), F32),
            jax.ShapeDtypeStruct((rows, 128), F32),
        ],
        input_output_aliases=aliases,
        compiler_params=pltpu.CompilerParams(vmem_limit_bytes=24 * 2**20),
        cost_estimate=cost(8 * rows * width * hidden, 8 * width * hidden),
        name="gate_up",
    )(blocks, *operands)


def down_block(width):
    return 512 if width % 512 == 0 else width


def last_gate_up_call(blocks, xa, xb, gain, gate_w, up_w, carried, down_w):
    rows, width = xa.shape
    hidden, total = gate_w.shape[1], gate_w.shape[2]
    size = rows_block(hidden, 264)
    steps = hidden // size
    cols = down_block(width)
    halves = width // cols

    def kernel(at, *refs):
        xa_ref, xb_ref, gain_a, gain_b, gate_a, gate_b, up_a, up_b = refs[:8]
        gate_in, up_in, parts_in, down_ref = refs[8:12]
        h_ref, theirs_ref, mine_ref, xg_ref, scale_ref, ht_ref = refs[12:]
        step = pl.program_id(0)

        @pl.when(step == 0)
        def _():
            parts = scaled_rows(xa_ref, xb_ref, gain_a, gain_b, xg_ref) + parts_in[...]
            mean = jnp.sum(parts, axis=-1, keepdims=True) * (1.0 / total)
            scale = jnp.broadcast_to(lax.rsqrt(mean + 1e-06), (rows, 128))
            scale_ref[...] = jnp.transpose(scale)[:8]

        @pl.when(step < steps)
        def _():
            gate, up = sums_of(xg_ref, gate_a, gate_b, up_a, up_b)
            scale = scale_ref[0:1, :]
            gate = (gate_in[...] + gate) * scale
            up = (up_in[...] + up) * scale
            value = gate / (1.0 + jnp.exp(-gate)) * up
            ht_ref[pl.ds(pl.multiple_of(step * size, 8), size), :] = value

        @pl.when(step == steps)
        def _():
            h_ref[...] = jnp.transpose(ht_ref[...]).astype(BF)

        @pl.when(step >= steps)
        def _():
            out = jnp.dot(h_ref[...], down_ref[0], preferred_element_type=F32)

            @pl.when(step < steps + halves)
            def _():
                theirs_ref[...] = out.astype(BF)

            @pl.when(step >= steps + halves)
            def _():
                mine_ref[...] = out

    up_to = lambda i: jnp.minimum(i, steps - 1)
    past = lambda i: jnp.maximum(i - steps, 0)
    whole = lambda shape: pl.BlockSpec(shape, lambda i, at: (0,) * len(shape))
    gain_spec = lambda n: pl.BlockSpec((1, width), lambda i, at: (0, at[n]))
    w_spec = lambda n: pl.BlockSpec((1, size, width), lambda i, at: (0, up_to(i), at[n]))
    sums = pl.BlockSpec((size, rows), lambda i, at: (up_to(i), 0))

    def down_at(i, at):
        j = past(i)
        return (0, 0, jnp.where(j < halves, at[2] * halves + j, at[3] * halves + j - halves))

    in_specs = [whole((rows, width))] * 2 + [gain_spec(0), gain_spec(1)]
    in_specs += [w_spec(0), w_spec(1), w_spec(0), w_spec(1), sums, sums, whole((rows, 128))]
    in_specs += [pl.BlockSpec((1, hidden, cols), down_at)]
    return pl.pallas_call(
        kernel,
        grid_spec=pltpu.PrefetchScalarGridSpec(
            num_scalar_prefetch=1,
            grid=(steps + 2 * halves,),
            in_specs=in_specs,
            out_specs=[
                whole((rows, hidden)),
                pl.BlockSpec((rows, cols), lambda i, at: (0, jnp.minimum(past(i), halves - 1))),
                pl.BlockSpec((rows, cols), lambda i, at: (0, jnp.maximum(past(i) - halves, 0))),
            ],
            scratch_shapes=[
                pltpu.VMEM((rows, 2 * width), BF),
                pltpu.VMEM((8, rows), F32),
                pltpu.VMEM((hidden, rows), F32),
            ],
        ),
        out_shape=[
            jax.ShapeDtypeStruct((rows, hidden), BF),
            jax.ShapeDtypeStruct((rows, width), BF),
            jax.ShapeDtypeStruct((rows, width), F32),
        ],
        compiler_params=pltpu.CompilerParams(vmem_limit_bytes=32 * 2**20),
        cost_estimate=cost(12 * rows * width * hidden, 12 * width * hidden),
        name="gate_up_down",
    )(blocks, xa, xb, gain, gain, gate_w, gate_w, up_w, up_w, *carried, down_w)


def down_call(blocks, h, down_w, width):
    rows, hidden = h.shape
    cols = down_block(width)
    halves = width // cols

    def kernel(at, h_ref, down_ref, theirs_ref, mine_ref):
        step = pl.program_id(0)
        out = jnp.dot(h_ref[...], down_ref[0], preferred_element_type=F32)

        @pl.when(step < halves)
        def _():
            theirs_ref[...] = out.astype(BF)

        @pl.when(step >= halves)
        def _():
            mine_ref[...] = out

    def down_at(i, at):
        return (0, 0, jnp.where(i < halves, at[0] * halves + i, at[1] * halves + i - halves))

    return pl.pallas_call(
        kernel,
        grid_spec=pltpu.PrefetchScalarGridSpec(
            num_scalar_prefetch=1,
            grid=(2 * halves,),
            in_specs=[
                pl.BlockSpec((rows, hidden), lambda i, at: (0, 0)),
                pl.BlockSpec((1, hidden, cols), down_at),
            ],
            out_specs=[
                pl.BlockSpec((rows, cols), lambda i, at: (0, jnp.minimum(i, halves - 1))),
                pl.BlockSpec((rows, cols), lambda i, at: (0, jnp.maximum(i - halves, 0))),
            ],
        ),
        out_shape=[
            jax.ShapeDtypeStruct((rows, width), BF),
            jax.ShapeDtypeStruct((rows, width), F32),
        ],
        compiler_params=pltpu.CompilerParams(vmem_limit_bytes=16 * 2**20),
        cost_estimate=cost(4 * rows * width * hidden, 4 * width * hidden),
        name="down",
    )(blocks, h, down_w)


def audio_rows(enc_states, ln_gain, ln_bias):
    local_clips, frame_len, enc_width = enc_states.shape
    clip_rows = frame_len // 2
    pairs = enc_states.astype(F32).reshape(local_clips, clip_rows, 2, enc_width)
    pooled = 0.5 * (pairs[:, :, 0] + pairs[:, :, 1])
    centre = jnp.mean(pooled, axis=-1, keepdims=True)
    centred = pooled - centre
    spread = jnp.mean(centred * centred, axis=-1, keepdims=True)
    audio_ln = (centred * lax.rsqrt(spread + 1e-05) * ln_gain + ln_bias).astype(BF)
    return audio_ln.reshape(local_clips * clip_rows, enc_width)


def embedded_rows(gathered, clip_rows, clip_frames, clip_offset, w_proj, proj_bias, text_embed):
    tokens, micro, feat_local = text_embed.shape
    slots = tokens * micro
    summed = jnp.dot(gathered, w_proj, preferred_element_type=F32)
    projected = (summed + proj_bias).astype(BF)
    within = jnp.arange(clip_rows, dtype=jnp.int32)
    live = within[None, :] * 2 < clip_frames[:, None]
    spot = clip_offset[:, None] + within[None, :]
    target = jnp.where(live, spot % tokens * micro + spot // tokens, slots).reshape(-1)
    match = jnp.arange(slots, dtype=jnp.int32)[:, None] == target[None, :]
    placed = jnp.dot(match.astype(BF), projected, preferred_element_type=F32).astype(BF)
    flags = jnp.any(match, axis=1, keepdims=True)
    return jnp.where(flags, placed, text_embed.reshape(slots, feat_local))


def ring_program(
    enc_states, clip_frames, clip_offset, ln_gain, ln_bias, w_proj, proj_bias, text_embed,
    norm_gain, w_gate, w_up, w_down,
):
    sections, parts = lax.axis_size("section"), lax.axis_size("fsdp")
    chips = parts // CORES
    both = ("section", "fsdp")
    section, part = lax.axis_index("section"), lax.axis_index("fsdp")
    chip, core = part // CORES, part % CORES
    tokens, micro, width = text_embed.shape
    rows = tokens * micro

    def place(sec, ch, co):
        return sec * parts + ch % chips * CORES + co

    everyone = [(ch, co) for ch in range(chips) for co in range(CORES)]

    def move(value, source, target, step):
        return lax.ppermute(
            value, both, [(place(source, ch, co), place(target, ch + step, co)) for ch, co in everyone]
        )

    def swap(value, sec):
        return lax.ppermute(
            value, both, [(place(sec, ch, co), place(sec, ch, 1 - co)) for ch, co in everyone]
        )

    def mine_theirs(ch):
        at = (ch + 2 * chips) % chips * CORES
        return [at + core, at + 1 - core]

    gathered = audio_rows(enc_states, ln_gain, ln_bias)
    span = 1
    while span < parts:
        got = lax.ppermute(gathered, "fsdp", [(i, i ^ span) for i in range(parts)])
        low = (part // span) % 2 == 0
        gathered = jnp.concatenate(
            [jnp.where(low, gathered, got), jnp.where(low, got, gathered)], axis=0
        )
        span *= 2
    clip_rows = enc_states.shape[1] // 2
    stream = embedded_rows(
        gathered, clip_rows, clip_frames, clip_offset, w_proj, proj_bias, text_embed
    )
    out_rows = rows // sections
    for stage in range(sections):
        ring_part = stream
        carried = None
        for step in range(chips):
            other = swap(ring_part, stage)
            following = move(ring_part, stage, stage, 1) if step + 1 < chips else None
            blocks = mine_theirs(chip - step)
            if step + 1 < chips:
                carried = gate_up_call(
                    jnp.stack(blocks), ring_part, other, norm_gain, w_gate, w_up, carried
                )
            else:
                ahead = mine_theirs(chip - 1)
                blocks = jnp.stack(blocks + [ahead[1], ahead[0]])
                h, theirs, mine = last_gate_up_call(
                    blocks, ring_part, other, norm_gain, w_gate, w_up, carried, w_down
                )
            ring_part = following
        running = None
        for step in range(chips):
            if step:
                at = mine_theirs(chip - 1 - step)
                theirs, mine = down_call(jnp.stack([at[1], at[0]]), h, w_down, width)
            here = mine + swap(theirs, stage).astype(F32)
            if step + 1 < chips:
                if running is not None:
                    here = here + move(running, stage, stage, 1).astype(F32)
                running = here.astype(BF)
        own = (here + stream.astype(F32)).astype(BF)
        if stage + 1 < sections:
            stream = (
                move(own, stage, stage + 1, 0).astype(F32)
                + move(running, stage, stage + 1, 1).astype(F32)
            ).astype(BF)
    out = 0.0
    for target in range(sections):
        block = slice(target * out_rows, (target + 1) * out_rows)
        if target == sections - 1:
            kept = jnp.where(section == target, own[block], 0).astype(F32)
        else:
            kept = move(own[block], sections - 1, target, 0).astype(F32)
        out = out + kept + move(running[block], sections - 1, target, 1).astype(F32)
    return out.astype(BF).reshape(tokens // sections, micro, width)


def general_program(
    enc_states, clip_frames, clip_offset, ln_gain, ln_bias, w_proj, proj_bias, text_embed,
    norm_gain, w_gate, w_up, w_down,
):
    sections = lax.axis_size("section")
    section = lax.axis_index("section")
    tokens, micro, width = text_embed.shape
    rows = tokens * micro
    gathered = lax.all_gather(
        audio_rows(enc_states, ln_gain, ln_bias), "fsdp", axis=0, tiled=True
    )
    clip_rows = enc_states.shape[1] // 2
    stream = embedded_rows(
        gathered, clip_rows, clip_frames, clip_offset, w_proj, proj_bias, text_embed
    )
    gate_w, up_w, down_w = w_gate[0], w_up[0], w_down[0]
    for stage in range(sections):
        whole = lax.all_gather(stream, "fsdp", axis=1, tiled=True)
        values = whole.astype(F32)
        scale = lax.rsqrt(jnp.mean(values * values, axis=-1, keepdims=True) + 1e-06)
        normed = (values * scale * norm_gain).astype(BF)
        gate = lax.dot_general(normed, gate_w, ROWS_BOTH, preferred_element_type=F32)
        up = lax.dot_general(normed, up_w, ROWS_BOTH, preferred_element_type=F32)
        hidden = (jax.nn.silu(gate) * up).astype(BF)
        summed = jnp.dot(hidden, down_w, preferred_element_type=F32)
        branch = lax.psum_scatter(summed, "fsdp", scatter_dimension=1, tiled=True)
        stream = (stream.astype(F32) + branch).astype(BF)
        if stage + 1 < sections:
            stream = lax.ppermute(stream, "section", [(stage, stage + 1)])
    out_rows = rows // sections
    out = 0.0
    for target in range(sections):
        block = stream[target * out_rows : (target + 1) * out_rows]
        if target == sections - 1:
            out = out + jnp.where(section == target, block, 0).astype(F32)
        else:
            out = out + lax.ppermute(block, "section", [(sections - 1, target)]).astype(F32)
    return out.astype(BF).reshape(tokens // sections, micro, width)


def solution(mesh):
    placed = (
        P("fsdp", None, None),
        P(),
        P(),
        P(),
        P(),
        P(None, "fsdp"),
        P("fsdp"),
        P(None, None, "fsdp"),
        P("section", None),
        P("section", "fsdp", None),
        P("section", "fsdp", None),
        P("section", "fsdp", None),
    )
    chips = mesh.shape["fsdp"] // CORES
    small = chips <= MOST_CHIPS and chips & (chips - 1) == 0
    return jax.shard_map(
        ring_program if small else general_program,
        mesh=mesh,
        in_specs=placed,
        out_specs=P("section", None, "fsdp"),
        check_vma=False,
    )
```

```python
import jax
import jax.numpy as jnp
from jax import lax
from jax.experimental import pallas as pl
from jax.experimental.pallas import tpu as pltpu
from jax.sharding import PartitionSpec as P


BF = jnp.bfloat16
F32 = jnp.float32
ROWS_BOTH = (((1,), (1,)), ((), ()))
CORES = 2
LINE_CHIPS = 4


def rows_block(total, most):
    best = total
    for size in range(8, min(total, most) + 1, 8):
        if total % size == 0:
            best = size
    return best


def cost(flops, nbytes):
    return pl.CostEstimate(flops=flops, bytes_accessed=nbytes, transcendentals=0)


VMEM = pl.BlockSpec(memory_space=pltpu.VMEM)
HBM = pl.BlockSpec(memory_space=pltpu.HBM)


def place_on_line():
    part = lax.axis_index("fsdp")
    return part // CORES, part % CORES


def chunk_at(order, chip, chips):
    if order == 0:
        return chip
    if order == 1:
        return chip + 1 - 2 * (chip % 2)
    low = chip < chips // 2
    return jnp.where(low, order, chips - 1 - order)


def scaled_rows(xa_ref, xb_ref, gain_ref, xg_ref, chunk, core):
    width = xa_ref.shape[1]
    parts = 0.0
    for x_ref, at in ((xa_ref, core), (xb_ref, 1 - core)):
        values = x_ref[...].astype(F32)
        squares = values * values
        for start in range(0, width, 128):
            parts = parts + squares[:, start : start + 128]
        gain = gain_ref[:, pl.ds(pl.multiple_of((chunk * CORES + at) * width, 128), width)]
        xg_ref[:, pl.ds(pl.multiple_of(at * width, 128), width)] = (values * gain).astype(BF)
    return parts


def in_hbm(w):
    return pltpu.with_memory_space_constraint(w, pltpu.HBM)


SLOTS = 3


def streamed(gate_ref, up_ref, xg_ref, buf, sem, chunk, prepare, use):
    slots, _, size, wide = buf.shape
    pieces = gate_ref.shape[1] // size
    start = pl.multiple_of(chunk * wide, 128)

    def copies(i):
        return [
            pltpu.make_async_copy(
                w_ref.at[0, pl.ds(pl.multiple_of(i * size, 8), size), pl.ds(start, wide)],
                buf.at[i % slots, n],
                sem.at[i % slots, n],
            )
            for n, w_ref in enumerate((gate_ref, up_ref))
        ]

    for i in range(slots):
        for copy in copies(i):
            copy.start()
    prepare()

    def piece(i, _):
        sums = []
        for n, copy in enumerate(copies(i)):
            copy.wait()
            sums.append(
                lax.dot_general(
                    buf[i % slots, n], xg_ref[...], ROWS_BOTH, preferred_element_type=F32
                )
            )

        @pl.when(i + slots < pieces)
        def _():
            for copy in copies(i + slots):
                copy.start()

        use(pl.ds(pl.multiple_of(i * size, 8), size), *sums)
        return 0

    lax.fori_loop(0, pieces, piece, 0)


def stream_scratch(hidden, rows, wide):
    size = rows_block(hidden, 640)
    slots = min(SLOTS, hidden // size)
    return [
        pltpu.VMEM((rows, wide), BF),
        pltpu.VMEM((slots, 2, size, wide), BF),
        pltpu.SemaphoreType.DMA((slots, 2)),
    ]


def gate_up_call(order, chips, xa, xb, gain, gate_w, up_w, carried):
    rows, width = xa.shape
    hidden = gate_w.shape[1]
    wide = width * CORES
    first = carried is None

    def kernel(*refs):
        xa_ref, xb_ref, gain_ref, gate_ref, up_ref = refs[:5]
        if first:
            gate_out, up_out, parts_out, xg_ref, buf, sem, none_ref = refs[5:]
        else:
            gate_in, up_in, parts_in, gate_out, up_out, parts_out, xg_ref, buf, sem, _ = refs[5:]
        chip, core = place_on_line()
        chunk = chunk_at(order, chip, chips)

        def prepare():
            parts = scaled_rows(xa_ref, xb_ref, gain_ref, xg_ref, chunk, core)
            parts_out[...] = parts if first else parts_in[...] + parts
            if first:
                none_ref[...] = jnp.zeros_like(none_ref)

        def use(at, gate, up):
            gate_out[at] = (none_ref[0:1] if first else gate_in[at]) + gate
            up_out[at] = (none_ref[0:1] if first else up_in[at]) + up

        streamed(gate_ref, up_ref, xg_ref, buf, sem, chunk, prepare, use)

    operands = [xa, xb, gain, in_hbm(gate_w), in_hbm(up_w)] + ([] if first else list(carried))
    return pl.pallas_call(
        kernel,
        in_specs=[VMEM] * 3 + [HBM] * 2 + [VMEM] * (len(operands) - 5),
        out_specs=[VMEM] * 3,
        out_shape=[
            jax.ShapeDtypeStruct((hidden, rows), F32),
            jax.ShapeDtypeStruct((hidden, rows), F32),
            jax.ShapeDtypeStruct((rows, 128), F32),
        ],
        scratch_shapes=stream_scratch(hidden, rows, wide) + [pltpu.VMEM((8, rows), F32)],
        input_output_aliases={} if first else {5: 0, 6: 1, 7: 2},
        compiler_params=pltpu.CompilerParams(vmem_limit_bytes=24 * 2**20),
        cost_estimate=cost(4 * rows * wide * hidden, 4 * wide * hidden),
        name="gate_up",
    )(*operands)


def down_copies(orders, chips, down_ref, buf, sem):
    _, hidden, width = buf.shape
    size = rows_block(hidden, 640)
    chip, core = place_on_line()
    halves = [
        (chunk_at(order, chip, chips) * CORES + at, order)
        for order in orders
        for at in (1 - core, core)
    ]
    return [
        [
            pltpu.make_async_copy(
                down_ref.at[
                    0, pl.ds(start, size), pl.ds(pl.multiple_of(at * width, 128), width)
                ],
                buf.at[n, pl.ds(start, size)],
                sem.at[n, start // size],
            )
            for start in range(0, hidden, size)
        ]
        for n, (at, _) in enumerate(halves)
    ]


def down_pairs(halves, h_ref, buf, none_ref, out_refs):
    none_ref[...] = jnp.zeros_like(none_ref)
    for n, (copies, out_ref) in enumerate(zip(halves, out_refs)):
        for copy in copies:
            copy.wait()
        out = jnp.dot(h_ref[...], buf[n], preferred_element_type=F32)
        out_ref[...] = (out + none_ref[0:1]).astype(out_ref.dtype)


def down_scratch(hidden, width, count):
    return [
        pltpu.VMEM((count, hidden, width), BF),
        pltpu.SemaphoreType.DMA((count, hidden // rows_block(hidden, 640))),
        pltpu.VMEM((8, width), F32),
    ]


def last_gate_up_call(order, chips, xa, xb, gain, gate_w, up_w, carried, down_w):
    rows, width = xa.shape
    hidden, total = down_w.shape[1:]
    wide = width * CORES

    def kernel(*refs):
        xa_ref, xb_ref, gain_ref, gate_ref, up_ref, gate_in, up_in, parts_in, down_ref = refs[:9]
        h_ref, theirs_ref, mine_ref, xg_ref, buf, sem, ht_ref, scale_ref = refs[9:17]
        down_buf, down_sem, none_ref = refs[17:]
        chip, core = place_on_line()
        chunk = chunk_at(order, chip, chips)

        down = down_copies([order], chips, down_ref, down_buf, down_sem)

        def prepare():
            for copy in sum(down, []):
                copy.start()
            parts = scaled_rows(xa_ref, xb_ref, gain_ref, xg_ref, chunk, core) + parts_in[...]
            mean = jnp.sum(parts, axis=-1, keepdims=True) * (1.0 / total)
            scale = jnp.broadcast_to(lax.rsqrt(mean + 1e-06), (rows, 128))
            scale_ref[...] = jnp.transpose(scale)[:8]

        def use(at, gate, up):
            scale = scale_ref[0:1]
            gate = (gate_in[at] + gate) * scale
            up = (up_in[at] + up) * scale
            ht_ref[at] = gate / (1.0 + jnp.exp(-gate)) * up

        streamed(gate_ref, up_ref, xg_ref, buf, sem, chunk, prepare, use)
        h_ref[...] = jnp.transpose(ht_ref[...]).astype(BF)
        down_pairs(down, h_ref, down_buf, none_ref, (theirs_ref, mine_ref))

    return pl.pallas_call(
        kernel,
        in_specs=[VMEM] * 3 + [HBM] * 2 + [VMEM] * 3 + [HBM],
        out_specs=[VMEM] * 3,
        out_shape=[
            jax.ShapeDtypeStruct((rows, hidden), BF),
            jax.ShapeDtypeStruct((rows, width), BF),
            jax.ShapeDtypeStruct((rows, width), F32),
        ],
        scratch_shapes=stream_scratch(hidden, rows, wide)
        + [pltpu.VMEM((hidden, rows), F32), pltpu.VMEM((8, rows), F32)]
        + down_scratch(hidden, width, CORES),
        compiler_params=pltpu.CompilerParams(vmem_limit_bytes=36 * 2**20),
        cost_estimate=cost(6 * rows * wide * hidden, 6 * wide * hidden),
        name="gate_up_down",
    )(xa, xb, gain, in_hbm(gate_w), in_hbm(up_w), *carried, in_hbm(down_w))


def down_call(orders, chips, h, down_w, width):
    rows, hidden = h.shape
    count = CORES * len(orders)

    def kernel(h_ref, down_ref, *refs):
        buf, sem, none_ref = refs[count:]
        halves = down_copies(orders, chips, down_ref, buf, sem)
        for copy in sum(halves, []):
            copy.start()
        down_pairs(halves, h_ref, buf, none_ref, refs[:count])

    return pl.pallas_call(
        kernel,
        in_specs=[VMEM, HBM],
        out_specs=[VMEM] * count,
        out_shape=[jax.ShapeDtypeStruct((rows, width), (BF, F32)[n % 2]) for n in range(count)],
        scratch_shapes=down_scratch(hidden, width, count),
        compiler_params=pltpu.CompilerParams(vmem_limit_bytes=12 * len(orders) * 2**20),
        cost_estimate=cost(4 * rows * width * hidden, 4 * width * hidden),
        name="down",
    )(h, in_hbm(down_w))


def audio_rows(enc_states, ln_gain, ln_bias):
    local_clips, frame_len, enc_width = enc_states.shape
    clip_rows = frame_len // 2
    pairs = enc_states.astype(F32).reshape(local_clips, clip_rows, 2, enc_width)
    pooled = 0.5 * (pairs[:, :, 0] + pairs[:, :, 1])
    centre = jnp.mean(pooled, axis=-1, keepdims=True)
    centred = pooled - centre
    spread = jnp.mean(centred * centred, axis=-1, keepdims=True)
    audio_ln = (centred * lax.rsqrt(spread + 1e-05) * ln_gain + ln_bias).astype(BF)
    return audio_ln.reshape(local_clips * clip_rows, enc_width)


def embedded_rows(gathered, clip_rows, clip_frames, clip_offset, w_proj, proj_bias, text_embed):
    tokens, micro, feat_local = text_embed.shape
    slots = tokens * micro
    summed = jnp.dot(gathered, w_proj, preferred_element_type=F32)
    projected = (summed + proj_bias).astype(BF)
    within = jnp.arange(clip_rows, dtype=jnp.int32)
    live = within[None, :] * 2 < clip_frames[:, None]
    spot = clip_offset[:, None] + within[None, :]
    target = jnp.where(live, spot % tokens * micro + spot // tokens, slots).reshape(-1)
    match = jnp.arange(slots, dtype=jnp.int32)[:, None] == target[None, :]
    placed = jnp.dot(match.astype(BF), projected, preferred_element_type=F32).astype(BF)
    flags = jnp.any(match, axis=1, keepdims=True)
    return jnp.where(flags, placed, text_embed.reshape(slots, feat_local))


def line_program(
    enc_states, clip_frames, clip_offset, ln_gain, ln_bias, w_proj, proj_bias, text_embed,
    norm_gain, w_gate, w_up, w_down,
):
    sections, parts = lax.axis_size("section"), lax.axis_size("fsdp")
    chips = parts // CORES
    both = ("section", "fsdp")
    section, part = lax.axis_index("section"), lax.axis_index("fsdp")
    chip = part // CORES
    middle = (chip > 0) & (chip < chips - 1)
    tokens, micro, width = text_embed.shape
    rows = tokens * micro
    everyone = [
        (sec, ch, co) for sec in range(sections) for ch in range(chips) for co in range(CORES)
    ]

    def place(sec, ch, co):
        return sec % sections * parts + ch * CORES + co

    def send(value, target):
        return lax.ppermute(value, both, [(place(*at), place(*target(*at))) for at in everyone])

    def outer(ch):
        return ch ^ 1

    def inner(ch):
        return ch if ch in (0, chips - 1) else chips - 1 - ch

    def swap(value):
        return send(value, lambda sec, ch, co: (sec, ch, 1 - co))

    def to_outer(value):
        return send(value, lambda sec, ch, co: (sec, outer(ch), co))

    def to_inner(value):
        return send(value, lambda sec, ch, co: (sec, inner(ch), co))

    def on_own(value):
        return send(value, lambda sec, ch, co: (sec + 1, ch, co))

    def on_outer(value):
        return send(value, lambda sec, ch, co: (sec + 1, outer(ch), co))

    def on_inner(value):
        return send(
            value, lambda sec, ch, co: (sec + (inner(ch) != ch), inner(ch), co)
        )

    def after(value, *others):
        return lax.optimization_barrier((value, *others))[0]

    gathered = audio_rows(enc_states, ln_gain, ln_bias)
    span = 1
    while span < parts:
        got = lax.ppermute(gathered, "fsdp", [(i, i ^ span) for i in range(parts)])
        low = (part // span) % 2 == 0
        gathered = jnp.concatenate(
            [jnp.where(low, gathered, got), jnp.where(low, got, gathered)], axis=0
        )
        span *= 2
    clip_rows = enc_states.shape[1] // 2
    stream = embedded_rows(
        gathered, clip_rows, clip_frames, clip_offset, w_proj, proj_bias, text_embed
    )
    for stage in range(sections):
        outer_1 = to_outer(stream)
        inner_1 = to_inner(stream)
        outer_2 = to_outer(inner_1)
        inner_2 = to_inner(outer_1)
        outer_3 = to_outer(inner_2)
        taken = [
            stream,
            outer_1,
            jnp.where(middle, inner_1, outer_2),
            jnp.where(middle, inner_2, outer_3),
        ]
        carried = None
        for order in range(chips - 1):
            other = swap(taken[order])
            carried = gate_up_call(
                order, chips, taken[order], other, norm_gain, w_gate, w_up, carried
            )
        last = chips - 1
        h, theirs, mine = last_gate_up_call(
            last, chips, taken[last], swap(taken[last]), norm_gain, w_gate, w_up, carried,
            w_down,
        )
        far = (mine + swap(theirs).astype(F32)).astype(BF)
        far_outer = to_outer(far)
        theirs, mine, theirs_own, mine_own = down_call([2, 0], chips, h, w_down, width)
        near = (mine + swap(theirs).astype(F32)).astype(BF)
        own = (mine_own + swap(theirs_own).astype(F32) + stream.astype(F32)).astype(BF)
        far_sum = (far.astype(F32) + far_outer.astype(F32)).astype(BF)
        far_inner = to_inner(far_sum)
        near_outer = to_outer(after(near, far_outer))
        theirs, mine = down_call([1], chips, h, w_down, width)
        pair = mine + swap(theirs).astype(F32)
        near = (near.astype(F32) + near_outer.astype(F32)).astype(BF)
        pair = (pair + jnp.where(middle, far_inner, 0).astype(F32)).astype(BF)
        if stage + 1 < sections:
            stream = (
                on_own(own).astype(F32)
                + jnp.where(middle, on_inner(near), 0).astype(F32)
                + on_outer(pair).astype(F32)
            ).astype(BF)
    out = (
        own.astype(F32)
        + jnp.where(middle, to_inner(near), 0).astype(F32)
        + to_outer(pair).astype(F32)
    ).astype(BF)
    out_rows = rows // sections
    final = 0.0
    for target in range(sections):
        block = out[target * out_rows : (target + 1) * out_rows]
        if target == sections - 1:
            kept = block
        else:
            step = (target + 1) % sections
            kept = send(block, lambda sec, ch, co: (sec + step, ch, co))
        final = final + jnp.where(section == target, kept, 0).astype(F32)
    return final.astype(BF).reshape(tokens // sections, micro, width)


def general_program(
    enc_states, clip_frames, clip_offset, ln_gain, ln_bias, w_proj, proj_bias, text_embed,
    norm_gain, w_gate, w_up, w_down,
):
    sections = lax.axis_size("section")
    section = lax.axis_index("section")
    tokens, micro, width = text_embed.shape
    rows = tokens * micro
    gathered = lax.all_gather(
        audio_rows(enc_states, ln_gain, ln_bias), "fsdp", axis=0, tiled=True
    )
    clip_rows = enc_states.shape[1] // 2
    stream = embedded_rows(
        gathered, clip_rows, clip_frames, clip_offset, w_proj, proj_bias, text_embed
    )
    gate_w, up_w, down_w = w_gate[0], w_up[0], w_down[0]
    for stage in range(sections):
        whole = lax.all_gather(stream, "fsdp", axis=1, tiled=True)
        values = whole.astype(F32)
        scale = lax.rsqrt(jnp.mean(values * values, axis=-1, keepdims=True) + 1e-06)
        normed = (values * scale * norm_gain).astype(BF)
        gate = lax.dot_general(normed, gate_w, ROWS_BOTH, preferred_element_type=F32)
        up = lax.dot_general(normed, up_w, ROWS_BOTH, preferred_element_type=F32)
        hidden = (jax.nn.silu(gate) * up).astype(BF)
        summed = jnp.dot(hidden, down_w, preferred_element_type=F32)
        branch = lax.psum_scatter(summed, "fsdp", scatter_dimension=1, tiled=True)
        stream = (stream.astype(F32) + branch).astype(BF)
        if stage + 1 < sections:
            stream = lax.ppermute(stream, "section", [(stage, stage + 1)])
    out_rows = rows // sections
    out = 0.0
    for target in range(sections):
        block = stream[target * out_rows : (target + 1) * out_rows]
        if target == sections - 1:
            out = out + jnp.where(section == target, block, 0).astype(F32)
        else:
            out = out + lax.ppermute(block, "section", [(sections - 1, target)]).astype(F32)
    return out.astype(BF).reshape(tokens // sections, micro, width)


def solution(mesh):
    placed = (
        P("fsdp", None, None),
        P(),
        P(),
        P(),
        P(),
        P(None, "fsdp"),
        P("fsdp"),
        P(None, None, "fsdp"),
        P("section", None),
        P("section", "fsdp", None),
        P("section", "fsdp", None),
        P("section", "fsdp", None),
    )
    chips = mesh.shape["fsdp"] // CORES
    line = chips == LINE_CHIPS
    return jax.shard_map(
        line_program if line else general_program,
        mesh=mesh,
        in_specs=placed,
        out_specs=P("section", None, "fsdp"),
        check_vma=False,
    )
```

```python
import jax
import jax.numpy as jnp
from jax import lax
from jax.experimental import pallas as pl
from jax.experimental.pallas import tpu as pltpu
from jax.sharding import PartitionSpec as P


BF = jnp.bfloat16
F32 = jnp.float32
ROWS_BOTH = (((1,), (1,)), ((), ()))
CORES = 2
LINE_CHIPS = 4


def rows_block(total, most):
    best = total
    for size in range(8, min(total, most) + 1, 8):
        if total % size == 0:
            best = size
    return best


def cost(flops, nbytes):
    return pl.CostEstimate(flops=flops, bytes_accessed=nbytes, transcendentals=0)


VMEM = pl.BlockSpec(memory_space=pltpu.VMEM)
HBM = pl.BlockSpec(memory_space=pltpu.HBM)


def place_on_line():
    part = lax.axis_index("fsdp")
    return part // CORES, part % CORES


def chunk_at(order, chip):
    return chip ^ order


def taken_at(order, chip, chips):
    middle = (chip > 0) & (chip < chips - 1)
    return chip ^ (jnp.where(middle, 5 - order, order) if order > 1 else order)


def scaled_rows(xa_ref, xb_ref, gain_ref, xg_ref, chunk, core):
    width = xa_ref.shape[1]
    parts = 0.0
    for x_ref, at in ((xa_ref, core), (xb_ref, 1 - core)):
        values = x_ref[...].astype(F32)
        squares = values * values
        for start in range(0, width, 128):
            parts = parts + squares[:, start : start + 128]
        gain = gain_ref[:, pl.ds(pl.multiple_of((chunk * CORES + at) * width, 128), width)]
        xg_ref[:, pl.ds(pl.multiple_of(at * width, 128), width)] = (values * gain).astype(BF)
    return parts


def in_hbm(w):
    return pltpu.with_memory_space_constraint(w, pltpu.HBM)


SLOTS = 3
DOWN_COLS = 1024


def streamed(gate_ref, up_ref, xg_ref, buf, sem, chunk, prepare, use):
    slots, _, size, wide = buf.shape
    pieces = gate_ref.shape[1] // size
    start = pl.multiple_of(chunk * wide, 128)

    def copies(i):
        return [
            pltpu.make_async_copy(
                w_ref.at[0, pl.ds(pl.multiple_of(i * size, 8), size), pl.ds(start, wide)],
                buf.at[i % slots, n],
                sem.at[i % slots, n],
            )
            for n, w_ref in enumerate((gate_ref, up_ref))
        ]

    for i in range(slots):
        for copy in copies(i):
            copy.start()
    prepare()

    def piece(i, _):
        sums = []
        for n, copy in enumerate(copies(i)):
            copy.wait()
            sums.append(
                lax.dot_general(
                    buf[i % slots, n], xg_ref[...], ROWS_BOTH, preferred_element_type=F32
                )
            )

        @pl.when(i + slots < pieces)
        def _():
            for copy in copies(i + slots):
                copy.start()

        use(pl.ds(pl.multiple_of(i * size, 8), size), *sums)
        return 0

    lax.fori_loop(0, pieces, piece, 0)


def stream_scratch(hidden, rows, wide):
    size = rows_block(hidden, 640)
    slots = min(SLOTS, hidden // size)
    return [
        pltpu.VMEM((rows, wide), BF),
        pltpu.VMEM((slots, 2, size, wide), BF),
        pltpu.SemaphoreType.DMA((slots, 2)),
    ]


def gate_up_call(order, chips, xa, xb, gain, gate_w, up_w, carried):
    rows, width = xa.shape
    hidden = gate_w.shape[1]
    wide = width * CORES
    first = carried is None

    def kernel(*refs):
        xa_ref, xb_ref, gain_ref, gate_ref, up_ref = refs[:5]
        if first:
            gate_out, up_out, parts_out, xg_ref, buf, sem, none_ref = refs[5:]
        else:
            gate_in, up_in, parts_in, gate_out, up_out, parts_out, xg_ref, buf, sem, _ = refs[5:]
        chip, core = place_on_line()
        chunk = taken_at(order, chip, chips)

        def prepare():
            parts = scaled_rows(xa_ref, xb_ref, gain_ref, xg_ref, chunk, core)
            parts_out[...] = parts if first else parts_in[...] + parts
            if first:
                none_ref[...] = jnp.zeros_like(none_ref)

        def use(at, gate, up):
            gate_out[at] = (none_ref[0:1] if first else gate_in[at]) + gate
            up_out[at] = (none_ref[0:1] if first else up_in[at]) + up

        streamed(gate_ref, up_ref, xg_ref, buf, sem, chunk, prepare, use)

    operands = [xa, xb, gain, in_hbm(gate_w), in_hbm(up_w)] + ([] if first else list(carried))
    return pl.pallas_call(
        kernel,
        in_specs=[VMEM] * 3 + [HBM] * 2 + [VMEM] * (len(operands) - 5),
        out_specs=[VMEM] * 3,
        out_shape=[
            jax.ShapeDtypeStruct((hidden, rows), F32),
            jax.ShapeDtypeStruct((hidden, rows), F32),
            jax.ShapeDtypeStruct((rows, 128), F32),
        ],
        scratch_shapes=stream_scratch(hidden, rows, wide) + [pltpu.VMEM((8, rows), F32)],
        input_output_aliases={} if first else {5: 0, 6: 1, 7: 2},
        compiler_params=pltpu.CompilerParams(vmem_limit_bytes=24 * 2**20),
        cost_estimate=cost(4 * rows * wide * hidden, 4 * wide * hidden),
        name="gate_up",
    )(*operands)


def down_copies(orders, down_ref, buf, sem):
    _, hidden, width = buf.shape
    size = rows_block(hidden, 640)
    chip, core = place_on_line()
    halves = [
        (chunk_at(order, chip) * CORES + at, order)
        for order in orders
        for at in (1 - core, core)
    ]
    return [
        [
            pltpu.make_async_copy(
                down_ref.at[
                    0, pl.ds(start, size), pl.ds(pl.multiple_of(at * width, 128), width)
                ],
                buf.at[n, pl.ds(start, size)],
                sem.at[n, start // size],
            )
            for start in range(0, hidden, size)
        ]
        for n, (at, _) in enumerate(halves)
    ]


def down_pairs(halves, h_ref, buf, none_ref, out_refs):
    width = buf.shape[2]
    cols = none_ref.shape[1]
    none_ref[...] = jnp.zeros_like(none_ref)
    for n, (copies, out_ref) in enumerate(zip(halves, out_refs)):
        for copy in copies:
            copy.wait()

        def columns(i, _):
            at = pl.ds(pl.multiple_of(i * cols, 128), cols)
            out = jnp.dot(h_ref[...], buf[n, :, at], preferred_element_type=F32)
            out_ref[:, at] = (out + none_ref[0:1]).astype(out_ref.dtype)
            return 0

        lax.fori_loop(0, width // cols, columns, 0)


def down_scratch(hidden, width, count):
    return [
        pltpu.VMEM((count, hidden, width), BF),
        pltpu.SemaphoreType.DMA((count, hidden // rows_block(hidden, 640))),
        pltpu.VMEM((8, DOWN_COLS if width % DOWN_COLS == 0 else width), F32),
    ]


def last_gate_up_call(order, down_order, chips, xa, xb, gain, gate_w, up_w, carried, down_w):
    rows, width = xa.shape
    hidden, total = down_w.shape[1:]
    wide = width * CORES

    def kernel(*refs):
        xa_ref, xb_ref, gain_ref, gate_ref, up_ref, gate_in, up_in, parts_in, down_ref = refs[:9]
        h_ref, theirs_ref, mine_ref, xg_ref, buf, sem, ht_ref, scale_ref = refs[9:17]
        down_buf, down_sem, none_ref = refs[17:]
        chip, core = place_on_line()
        chunk = taken_at(order, chip, chips)

        down = down_copies([down_order], down_ref, down_buf, down_sem)

        def prepare():
            for copy in sum(down, []):
                copy.start()
            parts = scaled_rows(xa_ref, xb_ref, gain_ref, xg_ref, chunk, core) + parts_in[...]
            mean = jnp.sum(parts, axis=-1, keepdims=True) * (1.0 / total)
            scale = jnp.broadcast_to(lax.rsqrt(mean + 1e-06), (rows, 128))
            scale_ref[...] = jnp.transpose(scale)[:8]

        def use(at, gate, up):
            scale = scale_ref[0:1]
            gate = (gate_in[at] + gate) * scale
            up = (up_in[at] + up) * scale
            ht_ref[at] = gate / (1.0 + jnp.exp(-gate)) * up

        streamed(gate_ref, up_ref, xg_ref, buf, sem, chunk, prepare, use)
        h_ref[...] = jnp.transpose(ht_ref[...]).astype(BF)
        down_pairs(down, h_ref, down_buf, none_ref, (theirs_ref, mine_ref))

    return pl.pallas_call(
        kernel,
        in_specs=[VMEM] * 3 + [HBM] * 2 + [VMEM] * 3 + [HBM],
        out_specs=[VMEM] * 3,
        out_shape=[
            jax.ShapeDtypeStruct((rows, hidden), BF),
            jax.ShapeDtypeStruct((rows, width), BF),
            jax.ShapeDtypeStruct((rows, width), F32),
        ],
        scratch_shapes=stream_scratch(hidden, rows, wide)
        + [pltpu.VMEM((hidden, rows), F32), pltpu.VMEM((8, rows), F32)]
        + down_scratch(hidden, width, CORES),
        compiler_params=pltpu.CompilerParams(vmem_limit_bytes=36 * 2**20),
        cost_estimate=cost(6 * rows * wide * hidden, 6 * wide * hidden),
        name="gate_up_down",
    )(xa, xb, gain, in_hbm(gate_w), in_hbm(up_w), *carried, in_hbm(down_w))


def down_call(orders, h, down_w, width):
    rows, hidden = h.shape
    count = CORES * len(orders)

    def kernel(h_ref, down_ref, *refs):
        buf, sem, none_ref = refs[count:]
        halves = down_copies(orders, down_ref, buf, sem)
        for copy in sum(halves, []):
            copy.start()
        down_pairs(halves, h_ref, buf, none_ref, refs[:count])

    return pl.pallas_call(
        kernel,
        in_specs=[VMEM, HBM],
        out_specs=[VMEM] * count,
        out_shape=[jax.ShapeDtypeStruct((rows, width), (BF, F32)[n % 2]) for n in range(count)],
        scratch_shapes=down_scratch(hidden, width, count),
        compiler_params=pltpu.CompilerParams(vmem_limit_bytes=12 * len(orders) * 2**20),
        cost_estimate=cost(4 * rows * width * hidden, 4 * width * hidden),
        name="down",
    )(h, in_hbm(down_w))


def audio_rows(enc_states, ln_gain, ln_bias):
    local_clips, frame_len, enc_width = enc_states.shape
    clip_rows = frame_len // 2
    pairs = enc_states.astype(F32).reshape(local_clips, clip_rows, 2, enc_width)
    pooled = 0.5 * (pairs[:, :, 0] + pairs[:, :, 1])
    centre = jnp.mean(pooled, axis=-1, keepdims=True)
    centred = pooled - centre
    spread = jnp.mean(centred * centred, axis=-1, keepdims=True)
    audio_ln = (centred * lax.rsqrt(spread + 1e-05) * ln_gain + ln_bias).astype(BF)
    return audio_ln.reshape(local_clips * clip_rows, enc_width)


def embedded_rows(gathered, clip_rows, clip_frames, clip_offset, w_proj, proj_bias, text_embed):
    tokens, micro, feat_local = text_embed.shape
    slots = tokens * micro
    summed = jnp.dot(gathered, w_proj, preferred_element_type=F32)
    projected = (summed + proj_bias).astype(BF)
    within = jnp.arange(clip_rows, dtype=jnp.int32)
    live = within[None, :] * 2 < clip_frames[:, None]
    spot = clip_offset[:, None] + within[None, :]
    target = jnp.where(live, spot % tokens * micro + spot // tokens, slots).reshape(-1)
    match = jnp.arange(slots, dtype=jnp.int32)[:, None] == target[None, :]
    placed = jnp.dot(match.astype(BF), projected, preferred_element_type=F32).astype(BF)
    flags = jnp.any(match, axis=1, keepdims=True)
    return jnp.where(flags, placed, text_embed.reshape(slots, feat_local))


def line_program(
    enc_states, clip_frames, clip_offset, ln_gain, ln_bias, w_proj, proj_bias, text_embed,
    norm_gain, w_gate, w_up, w_down,
):
    sections, parts = lax.axis_size("section"), lax.axis_size("fsdp")
    chips = parts // CORES
    both = ("section", "fsdp")
    section, part = lax.axis_index("section"), lax.axis_index("fsdp")
    chip = part // CORES
    middle = (chip > 0) & (chip < chips - 1)
    tokens, micro, width = text_embed.shape
    rows = tokens * micro

    def exchange(value, order=0, over=0, other_core=0):
        bits = (over * chips + order) * CORES + other_core
        return lax.ppermute(value, both, [(at, at ^ bits) for at in range(sections * parts)])

    def swap(value):
        return exchange(value, other_core=1)

    def to_inner(value):
        across = (chips - 1) * CORES
        ends = (0, chips - 1)
        return lax.ppermute(
            value,
            "fsdp",
            [(at, at if at // CORES in ends else at ^ across) for at in range(parts)],
        )

    rows_here = audio_rows(enc_states, ln_gain, ln_bias)
    core = part % CORES
    beside = lax.ppermute(rows_here, "fsdp", [(i, i ^ 1) for i in range(parts)])
    chip_rows = jnp.concatenate([rows_here, beside], axis=0)
    gathered = [chip_rows]
    for shift in range(1, chips):
        hop = [(i, (i + shift * CORES) % parts) for i in range(parts)]
        gathered.append(lax.ppermute(chip_rows, "fsdp", hop))
    position = jnp.arange(parts, dtype=jnp.int32)
    source = (chip - position // CORES + chips) % chips * CORES + (core + position) % CORES
    pick = source[:, None] == position[None, :]

    def in_order(per_clip):
        local = per_clip.reshape(parts, -1)
        return jnp.sum(jnp.where(pick[:, :, None], local[None], 0), axis=1).reshape(-1)

    clip_rows = enc_states.shape[1] // 2
    stream = embedded_rows(
        jnp.concatenate(gathered, axis=0), clip_rows, in_order(clip_frames),
        in_order(clip_offset), w_proj, proj_bias, text_embed,
    )
    for stage in range(sections):
        last = chips - 1
        onward = stage ^ (stage + 1) if stage + 1 < sections else 0
        outer_1 = exchange(stream, 1)
        inner_1 = to_inner(stream)
        outer_2 = exchange(inner_1, 1)
        inner_2 = to_inner(outer_1)
        outer_3 = exchange(inner_2, 1)
        taken = [
            stream,
            outer_1,
            jnp.where(middle, inner_1, outer_2),
            jnp.where(middle, inner_2, outer_3),
        ]
        carried = None
        for order in range(last):
            other = swap(taken[order])
            carried = gate_up_call(
                order, chips, taken[order], other, norm_gain, w_gate, w_up, carried
            )
        h, theirs, mine = last_gate_up_call(
            last, 2, chips, taken[last], swap(taken[last]), norm_gain, w_gate, w_up, carried,
            w_down,
        )
        across = mine + swap(theirs).astype(F32)
        across = exchange(across.astype(BF), 1).astype(F32)
        sums = down_call([1, 3, 0], h, w_down, width)
        pair, mirrored, own = [
            mine + swap(theirs).astype(F32) for theirs, mine in zip(sums[::2], sums[1::2])
        ]
        pair = exchange(pair.astype(BF), 1).astype(F32)
        mirrored = exchange((mirrored + across).astype(BF), 3, onward).astype(F32)
        own = own + stream.astype(F32) + pair
        if onward:
            own = exchange(own.astype(BF), 0, onward).astype(F32)
        stream = (own + mirrored).astype(BF)
    out_rows = rows // sections
    final = 0.0
    for target in range(sections):
        block = stream[target * out_rows : (target + 1) * out_rows]
        if target == sections - 1:
            kept = block
        else:
            kept = exchange(block, over=target ^ (sections - 1))
        final = final + jnp.where(section == target, kept, 0).astype(F32)
    return final.astype(BF).reshape(tokens // sections, micro, width)


def general_program(
    enc_states, clip_frames, clip_offset, ln_gain, ln_bias, w_proj, proj_bias, text_embed,
    norm_gain, w_gate, w_up, w_down,
):
    sections = lax.axis_size("section")
    section = lax.axis_index("section")
    tokens, micro, width = text_embed.shape
    rows = tokens * micro
    gathered = lax.all_gather(
        audio_rows(enc_states, ln_gain, ln_bias), "fsdp", axis=0, tiled=True
    )
    clip_rows = enc_states.shape[1] // 2
    stream = embedded_rows(
        gathered, clip_rows, clip_frames, clip_offset, w_proj, proj_bias, text_embed
    )
    gate_w, up_w, down_w = w_gate[0], w_up[0], w_down[0]
    for stage in range(sections):
        whole = lax.all_gather(stream, "fsdp", axis=1, tiled=True)
        values = whole.astype(F32)
        scale = lax.rsqrt(jnp.mean(values * values, axis=-1, keepdims=True) + 1e-06)
        normed = (values * scale * norm_gain).astype(BF)
        gate = lax.dot_general(normed, gate_w, ROWS_BOTH, preferred_element_type=F32)
        up = lax.dot_general(normed, up_w, ROWS_BOTH, preferred_element_type=F32)
        hidden = (jax.nn.silu(gate) * up).astype(BF)
        summed = jnp.dot(hidden, down_w, preferred_element_type=F32)
        branch = lax.psum_scatter(summed, "fsdp", scatter_dimension=1, tiled=True)
        stream = (stream.astype(F32) + branch).astype(BF)
        if stage + 1 < sections:
            stream = lax.ppermute(stream, "section", [(stage, stage + 1)])
    out_rows = rows // sections
    out = 0.0
    for target in range(sections):
        block = stream[target * out_rows : (target + 1) * out_rows]
        if target == sections - 1:
            out = out + jnp.where(section == target, block, 0).astype(F32)
        else:
            out = out + lax.ppermute(block, "section", [(sections - 1, target)]).astype(F32)
    return out.astype(BF).reshape(tokens // sections, micro, width)


def solution(mesh):
    placed = (
        P("fsdp", None, None),
        P(),
        P(),
        P(),
        P(),
        P(None, "fsdp"),
        P("fsdp"),
        P(None, None, "fsdp"),
        P("section", None),
        P("section", "fsdp", None),
        P("section", "fsdp", None),
        P("section", "fsdp", None),
    )
    chips = mesh.shape["fsdp"] // CORES
    sections = mesh.shape["section"]
    line = chips == LINE_CHIPS and sections & (sections - 1) == 0
    return jax.shard_map(
        line_program if line else general_program,
        mesh=mesh,
        in_specs=placed,
        out_specs=P("section", None, "fsdp"),
        check_vma=False,
    )
```

```python
import jax
import jax.numpy as jnp
from jax import lax
from jax.experimental import pallas as pl
from jax.experimental.pallas import tpu as pltpu
from jax.sharding import PartitionSpec as P


BF = jnp.bfloat16
F32 = jnp.float32
ROWS_BOTH = (((1,), (1,)), ((), ()))
CORES = 2
LINE_CHIPS = 4


def rows_block(total, most):
    best = total
    for size in range(8, min(total, most) + 1, 8):
        if total % size == 0:
            best = size
    return best


def cost(flops, nbytes):
    return pl.CostEstimate(flops=flops, bytes_accessed=nbytes, transcendentals=0)


VMEM = pl.BlockSpec(memory_space=pltpu.VMEM)
HBM = pl.BlockSpec(memory_space=pltpu.HBM)


def place_on_line():
    part = lax.axis_index("fsdp")
    return part // CORES, part % CORES


def chunk_at(order, chip):
    return chip ^ order


def taken_at(order, chip, chips):
    middle = (chip > 0) & (chip < chips - 1)
    return chip ^ (jnp.where(middle, 5 - order, order) if order > 1 else order)


def scaled_rows(xa_ref, xb_ref, gain_ref, xg_ref, chunk, core):
    width = xa_ref.shape[1]
    parts = 0.0
    for x_ref, at in ((xa_ref, core), (xb_ref, 1 - core)):
        values = x_ref[...].astype(F32)
        squares = values * values
        for start in range(0, width, 128):
            parts = parts + squares[:, start : start + 128]
        gain = gain_ref[:, pl.ds(pl.multiple_of((chunk * CORES + at) * width, 128), width)]
        xg_ref[:, pl.ds(pl.multiple_of(at * width, 128), width)] = (values * gain).astype(BF)
    return parts


def in_hbm(w):
    return pltpu.with_memory_space_constraint(w, pltpu.HBM)


SLOTS = 3
DOWN_COLS = 512


def streamed(gate_ref, up_ref, xg_ref, buf, sem, chunk, prepare, use):
    slots, _, size, wide = buf.shape
    pieces = gate_ref.shape[1] // size
    start = pl.multiple_of(chunk * wide, 128)

    def copies(i):
        return [
            pltpu.make_async_copy(
                w_ref.at[0, pl.ds(pl.multiple_of(i * size, 8), size), pl.ds(start, wide)],
                buf.at[i % slots, n],
                sem.at[i % slots, n],
            )
            for n, w_ref in enumerate((gate_ref, up_ref))
        ]

    for i in range(slots):
        for copy in copies(i):
            copy.start()
    prepare()

    def piece(i, _):
        sums = []
        for n, copy in enumerate(copies(i)):
            copy.wait()
            sums.append(
                lax.dot_general(
                    buf[i % slots, n], xg_ref[...], ROWS_BOTH, preferred_element_type=F32
                )
            )

        @pl.when(i + slots < pieces)
        def _():
            for copy in copies(i + slots):
                copy.start()

        use(pl.ds(pl.multiple_of(i * size, 8), size), *sums)
        return 0

    lax.fori_loop(0, pieces, piece, 0)


def stream_scratch(hidden, rows, wide):
    size = rows_block(hidden, 640)
    slots = min(SLOTS, hidden // size)
    return [
        pltpu.VMEM((rows, wide), BF),
        pltpu.VMEM((slots, 2, size, wide), BF),
        pltpu.SemaphoreType.DMA((slots, 2)),
    ]


def gate_up_call(order, chips, xa, xb, gain, gate_w, up_w, carried):
    rows, width = xa.shape
    hidden = gate_w.shape[1]
    wide = width * CORES
    first = carried is None

    def kernel(*refs):
        xa_ref, xb_ref, gain_ref, gate_ref, up_ref = refs[:5]
        if first:
            gate_out, up_out, parts_out, xg_ref, buf, sem, none_ref = refs[5:]
        else:
            gate_in, up_in, parts_in, gate_out, up_out, parts_out, xg_ref, buf, sem, _ = refs[5:]
        chip, core = place_on_line()
        chunk = taken_at(order, chip, chips)

        def prepare():
            parts = scaled_rows(xa_ref, xb_ref, gain_ref, xg_ref, chunk, core)
            parts_out[...] = parts if first else parts_in[...] + parts
            if first:
                none_ref[...] = jnp.zeros_like(none_ref)

        def use(at, gate, up):
            gate_out[at] = (none_ref[0:1] if first else gate_in[at]) + gate
            up_out[at] = (none_ref[0:1] if first else up_in[at]) + up

        streamed(gate_ref, up_ref, xg_ref, buf, sem, chunk, prepare, use)

    operands = [xa, xb, gain, in_hbm(gate_w), in_hbm(up_w)] + ([] if first else list(carried))
    return pl.pallas_call(
        kernel,
        in_specs=[VMEM] * 3 + [HBM] * 2 + [VMEM] * (len(operands) - 5),
        out_specs=[VMEM] * 3,
        out_shape=[
            jax.ShapeDtypeStruct((hidden, rows), F32),
            jax.ShapeDtypeStruct((hidden, rows), F32),
            jax.ShapeDtypeStruct((rows, 128), F32),
        ],
        scratch_shapes=stream_scratch(hidden, rows, wide) + [pltpu.VMEM((8, rows), F32)],
        input_output_aliases={} if first else {5: 0, 6: 1, 7: 2},
        compiler_params=pltpu.CompilerParams(vmem_limit_bytes=24 * 2**20),
        cost_estimate=cost(4 * rows * wide * hidden, 4 * wide * hidden),
        name="gate_up",
    )(*operands)


def down_copies(orders, down_ref, buf, sem):
    _, hidden, width = buf.shape
    size = rows_block(hidden, 640)
    chip, core = place_on_line()
    halves = [
        (chunk_at(order, chip) * CORES + at, order)
        for order in orders
        for at in (1 - core, core)
    ]
    return [
        [
            pltpu.make_async_copy(
                down_ref.at[
                    0, pl.ds(start, size), pl.ds(pl.multiple_of(at * width, 128), width)
                ],
                buf.at[n, pl.ds(start, size)],
                sem.at[n, start // size],
            )
            for start in range(0, hidden, size)
        ]
        for n, (at, _) in enumerate(halves)
    ]


def down_pairs(halves, h_ref, buf, none_ref, out_refs):
    width = buf.shape[2]
    cols = none_ref.shape[1]
    none_ref[...] = jnp.zeros_like(none_ref)
    for n, (copies, out_ref) in enumerate(zip(halves, out_refs)):
        for copy in copies:
            copy.wait()

        def columns(i, _):
            at = pl.ds(pl.multiple_of(i * cols, 128), cols)
            out = jnp.dot(h_ref[...], buf[n, :, at], preferred_element_type=F32)
            out_ref[:, at] = (out + none_ref[0:1]).astype(out_ref.dtype)
            return 0

        lax.fori_loop(0, width // cols, columns, 0)


def down_scratch(hidden, width, count):
    return [
        pltpu.VMEM((count, hidden, width), BF),
        pltpu.SemaphoreType.DMA((count, hidden // rows_block(hidden, 640))),
        pltpu.VMEM((8, DOWN_COLS if width % DOWN_COLS == 0 else width), F32),
    ]


def last_gate_up_call(order, down_order, chips, xa, xb, gain, gate_w, up_w, carried, down_w):
    rows, width = xa.shape
    hidden, total = down_w.shape[1:]
    wide = width * CORES

    def kernel(*refs):
        xa_ref, xb_ref, gain_ref, gate_ref, up_ref, gate_in, up_in, parts_in, down_ref = refs[:9]
        h_ref, theirs_ref, mine_ref, xg_ref, buf, sem, ht_ref, scale_ref = refs[9:17]
        down_buf, down_sem, none_ref = refs[17:]
        chip, core = place_on_line()
        chunk = taken_at(order, chip, chips)

        down = down_copies([down_order], down_ref, down_buf, down_sem)

        def prepare():
            for copy in sum(down, []):
                copy.start()
            parts = scaled_rows(xa_ref, xb_ref, gain_ref, xg_ref, chunk, core) + parts_in[...]
            mean = jnp.sum(parts, axis=-1, keepdims=True) * (1.0 / total)
            scale = jnp.broadcast_to(lax.rsqrt(mean + 1e-06), (rows, 128))
            scale_ref[...] = jnp.transpose(scale)[:8]

        def use(at, gate, up):
            scale = scale_ref[0:1]
            gate = (gate_in[at] + gate) * scale
            up = (up_in[at] + up) * scale
            ht_ref[at] = gate / (1.0 + jnp.exp(-gate)) * up

        streamed(gate_ref, up_ref, xg_ref, buf, sem, chunk, prepare, use)
        h_ref[...] = jnp.transpose(ht_ref[...]).astype(BF)
        down_pairs(down, h_ref, down_buf, none_ref, (theirs_ref, mine_ref))

    return pl.pallas_call(
        kernel,
        in_specs=[VMEM] * 3 + [HBM] * 2 + [VMEM] * 3 + [HBM],
        out_specs=[VMEM] * 3,
        out_shape=[
            jax.ShapeDtypeStruct((rows, hidden), BF),
            jax.ShapeDtypeStruct((rows, width), BF),
            jax.ShapeDtypeStruct((rows, width), F32),
        ],
        scratch_shapes=stream_scratch(hidden, rows, wide)
        + [pltpu.VMEM((hidden, rows), F32), pltpu.VMEM((8, rows), F32)]
        + down_scratch(hidden, width, CORES),
        compiler_params=pltpu.CompilerParams(vmem_limit_bytes=36 * 2**20),
        cost_estimate=cost(6 * rows * wide * hidden, 6 * wide * hidden),
        name="gate_up_down",
    )(xa, xb, gain, in_hbm(gate_w), in_hbm(up_w), *carried, in_hbm(down_w))


def down_call(orders, h, down_w, width):
    rows, hidden = h.shape
    count = CORES * len(orders)

    def kernel(h_ref, down_ref, *refs):
        buf, sem, none_ref = refs[count:]
        halves = down_copies(orders, down_ref, buf, sem)
        for copy in sum(halves, []):
            copy.start()
        down_pairs(halves, h_ref, buf, none_ref, refs[:count])

    return pl.pallas_call(
        kernel,
        in_specs=[VMEM, HBM],
        out_specs=[VMEM] * count,
        out_shape=[jax.ShapeDtypeStruct((rows, width), (BF, F32)[n % 2]) for n in range(count)],
        scratch_shapes=down_scratch(hidden, width, count),
        compiler_params=pltpu.CompilerParams(vmem_limit_bytes=12 * len(orders) * 2**20),
        cost_estimate=cost(4 * rows * width * hidden, 4 * width * hidden),
        name="down",
    )(h, in_hbm(down_w))


def audio_rows(enc_states, ln_gain, ln_bias):
    local_clips, frame_len, enc_width = enc_states.shape
    clip_rows = frame_len // 2
    pairs = enc_states.astype(F32).reshape(local_clips, clip_rows, 2, enc_width)
    pooled = 0.5 * (pairs[:, :, 0] + pairs[:, :, 1])
    centre = jnp.mean(pooled, axis=-1, keepdims=True)
    centred = pooled - centre
    spread = jnp.mean(centred * centred, axis=-1, keepdims=True)
    audio_ln = (centred * lax.rsqrt(spread + 1e-05) * ln_gain + ln_bias).astype(BF)
    return audio_ln.reshape(local_clips * clip_rows, enc_width)


def embedded_rows(gathered, clip_rows, clip_frames, clip_offset, w_proj, proj_bias, text_embed):
    tokens, micro, feat_local = text_embed.shape
    slots = tokens * micro
    summed = jnp.dot(gathered, w_proj, preferred_element_type=F32)
    projected = (summed + proj_bias).astype(BF)
    within = jnp.arange(clip_rows, dtype=jnp.int32)
    live = within[None, :] * 2 < clip_frames[:, None]
    spot = clip_offset[:, None] + within[None, :]
    target = jnp.where(live, spot % tokens * micro + spot // tokens, slots).reshape(-1)
    match = jnp.arange(slots, dtype=jnp.int32)[:, None] == target[None, :]
    placed = jnp.dot(match.astype(BF), projected, preferred_element_type=F32).astype(BF)
    flags = jnp.any(match, axis=1, keepdims=True)
    return jnp.where(flags, placed, text_embed.reshape(slots, feat_local))


def line_program(
    enc_states, clip_frames, clip_offset, ln_gain, ln_bias, w_proj, proj_bias, text_embed,
    norm_gain, w_gate, w_up, w_down,
):
    sections, parts = lax.axis_size("section"), lax.axis_size("fsdp")
    chips = parts // CORES
    both = ("section", "fsdp")
    section, part = lax.axis_index("section"), lax.axis_index("fsdp")
    chip = part // CORES
    middle = (chip > 0) & (chip < chips - 1)
    tokens, micro, width = text_embed.shape
    rows = tokens * micro

    def exchange(value, order=0, over=0, other_core=0):
        bits = (over * chips + order) * CORES + other_core
        return lax.ppermute(value, both, [(at, at ^ bits) for at in range(sections * parts)])

    def swap(value):
        return exchange(value, other_core=1)

    def to_inner(value):
        across = (chips - 1) * CORES
        ends = (0, chips - 1)
        return lax.ppermute(
            value,
            "fsdp",
            [(at, at if at // CORES in ends else at ^ across) for at in range(parts)],
        )

    rows_here = audio_rows(enc_states, ln_gain, ln_bias)
    beside = lax.ppermute(rows_here, "fsdp", [(i, i ^ 1) for i in range(parts)])
    chip_rows = jnp.concatenate([rows_here, beside], axis=0)
    gathered = [chip_rows]
    for shift in range(1, chips):
        hop = [(i, i ^ (shift * CORES)) for i in range(parts)]
        gathered.append(lax.ppermute(chip_rows, "fsdp", hop))
    position = jnp.arange(parts, dtype=jnp.int32)
    source = part ^ position
    pick = source[:, None] == position[None, :]

    def in_order(per_clip):
        local = per_clip.reshape(parts, -1)
        return jnp.sum(jnp.where(pick[:, :, None], local[None], 0), axis=1).reshape(-1)

    clip_rows = enc_states.shape[1] // 2
    stream = embedded_rows(
        jnp.concatenate(gathered, axis=0), clip_rows, in_order(clip_frames),
        in_order(clip_offset), w_proj, proj_bias, text_embed,
    )
    for stage in range(sections):
        last = chips - 1
        onward = stage ^ (stage + 1) if stage + 1 < sections else 0
        outer_1 = exchange(stream, 1)
        inner_1 = to_inner(stream)
        outer_2 = exchange(inner_1, 1)
        inner_2 = to_inner(outer_1)
        outer_3 = exchange(inner_2, 1)
        taken = [
            stream,
            outer_1,
            jnp.where(middle, inner_1, outer_2),
            jnp.where(middle, inner_2, outer_3),
        ]
        carried = None
        for order in range(last):
            other = swap(taken[order])
            carried = gate_up_call(
                order, chips, taken[order], other, norm_gain, w_gate, w_up, carried
            )
        h, theirs, mine = last_gate_up_call(
            last, 2, chips, taken[last], swap(taken[last]), norm_gain, w_gate, w_up, carried,
            w_down,
        )
        across = mine + swap(theirs).astype(F32)
        across = exchange(across.astype(BF), 1).astype(F32)
        sums = down_call([1, 3], h, w_down, width)
        pair, mirrored = [
            mine + swap(theirs).astype(F32) for theirs, mine in zip(sums[::2], sums[1::2])
        ]
        pair = exchange(pair.astype(BF), 1).astype(F32)
        mirrored = exchange((mirrored + across).astype(BF), 3, onward).astype(F32)
        theirs, mine = down_call([0], h, w_down, width)
        own = mine + swap(theirs).astype(F32)
        own = own + stream.astype(F32) + pair
        if onward:
            own = exchange(own.astype(BF), 0, onward).astype(F32)
        stream = (own + mirrored).astype(BF)
    out_rows = rows // sections
    final = 0.0
    for target in range(sections):
        block = stream[target * out_rows : (target + 1) * out_rows]
        if target == sections - 1:
            kept = block
        else:
            kept = exchange(block, over=target ^ (sections - 1))
        final = final + jnp.where(section == target, kept, 0).astype(F32)
    return final.astype(BF).reshape(tokens // sections, micro, width)


def general_program(
    enc_states, clip_frames, clip_offset, ln_gain, ln_bias, w_proj, proj_bias, text_embed,
    norm_gain, w_gate, w_up, w_down,
):
    sections = lax.axis_size("section")
    section = lax.axis_index("section")
    tokens, micro, width = text_embed.shape
    rows = tokens * micro
    gathered = lax.all_gather(
        audio_rows(enc_states, ln_gain, ln_bias), "fsdp", axis=0, tiled=True
    )
    clip_rows = enc_states.shape[1] // 2
    stream = embedded_rows(
        gathered, clip_rows, clip_frames, clip_offset, w_proj, proj_bias, text_embed
    )
    gate_w, up_w, down_w = w_gate[0], w_up[0], w_down[0]
    for stage in range(sections):
        whole = lax.all_gather(stream, "fsdp", axis=1, tiled=True)
        values = whole.astype(F32)
        scale = lax.rsqrt(jnp.mean(values * values, axis=-1, keepdims=True) + 1e-06)
        normed = (values * scale * norm_gain).astype(BF)
        gate = lax.dot_general(normed, gate_w, ROWS_BOTH, preferred_element_type=F32)
        up = lax.dot_general(normed, up_w, ROWS_BOTH, preferred_element_type=F32)
        hidden = (jax.nn.silu(gate) * up).astype(BF)
        summed = jnp.dot(hidden, down_w, preferred_element_type=F32)
        branch = lax.psum_scatter(summed, "fsdp", scatter_dimension=1, tiled=True)
        stream = (stream.astype(F32) + branch).astype(BF)
        if stage + 1 < sections:
            stream = lax.ppermute(stream, "section", [(stage, stage + 1)])
    out_rows = rows // sections
    out = 0.0
    for target in range(sections):
        block = stream[target * out_rows : (target + 1) * out_rows]
        if target == sections - 1:
            out = out + jnp.where(section == target, block, 0).astype(F32)
        else:
            out = out + lax.ppermute(block, "section", [(sections - 1, target)]).astype(F32)
    return out.astype(BF).reshape(tokens // sections, micro, width)


def solution(mesh):
    placed = (
        P("fsdp", None, None),
        P(),
        P(),
        P(),
        P(),
        P(None, "fsdp"),
        P("fsdp"),
        P(None, None, "fsdp"),
        P("section", None),
        P("section", "fsdp", None),
        P("section", "fsdp", None),
        P("section", "fsdp", None),
    )
    chips = mesh.shape["fsdp"] // CORES
    sections = mesh.shape["section"]
    line = chips == LINE_CHIPS and sections & (sections - 1) == 0
    return jax.shard_map(
        line_program if line else general_program,
        mesh=mesh,
        in_specs=placed,
        out_specs=P("section", None, "fsdp"),
        check_vma=False,
    )
```

```python
import jax
import jax.numpy as jnp
from jax import lax
from jax.experimental import pallas as pl
from jax.experimental.pallas import tpu as pltpu
from jax.sharding import PartitionSpec as P


BF = jnp.bfloat16
F32 = jnp.float32
ROWS_BOTH = (((1,), (1,)), ((), ()))
CORES = 2
LINE_CHIPS = 4


def rows_block(total, most):
    best = total
    for size in range(8, min(total, most) + 1, 8):
        if total % size == 0:
            best = size
    return best


def cost(flops, nbytes):
    return pl.CostEstimate(flops=flops, bytes_accessed=nbytes, transcendentals=0)


VMEM = pl.BlockSpec(memory_space=pltpu.VMEM)
HBM = pl.BlockSpec(memory_space=pltpu.HBM)


def place_on_line():
    part = lax.axis_index("fsdp")
    return part // CORES, part % CORES


def chunk_at(order, chip):
    return chip ^ order


def scaled_rows(xa_ref, xb_ref, gain_ref, xg_ref, chunk, core):
    width = xa_ref.shape[1]
    parts = 0.0
    for x_ref, at in ((xa_ref, core), (xb_ref, 1 - core)):
        values = x_ref[...].astype(F32)
        squares = values * values
        for start in range(0, width, 128):
            parts = parts + squares[:, start : start + 128]
        gain = gain_ref[:, pl.ds(pl.multiple_of((chunk * CORES + at) * width, 128), width)]
        xg_ref[:, pl.ds(pl.multiple_of(at * width, 128), width)] = (values * gain).astype(BF)
    return parts


def in_hbm(w):
    return pltpu.with_memory_space_constraint(w, pltpu.HBM)


SLOTS = 3
DOWN_COLS = 512


def streamed(gate_ref, up_ref, xg_ref, buf, sem, chunk, prepare, use):
    slots, _, size, wide = buf.shape
    pieces = gate_ref.shape[1] // size
    start = pl.multiple_of(chunk * wide, 128)

    def copies(i):
        return [
            pltpu.make_async_copy(
                w_ref.at[0, pl.ds(pl.multiple_of(i * size, 8), size), pl.ds(start, wide)],
                buf.at[i % slots, n],
                sem.at[i % slots, n],
            )
            for n, w_ref in enumerate((gate_ref, up_ref))
        ]

    for i in range(slots):
        for copy in copies(i):
            copy.start()
    prepare()

    def piece(i, _):
        sums = []
        for n, copy in enumerate(copies(i)):
            copy.wait()
            sums.append(
                lax.dot_general(
                    buf[i % slots, n], xg_ref[...], ROWS_BOTH, preferred_element_type=F32
                )
            )

        @pl.when(i + slots < pieces)
        def _():
            for copy in copies(i + slots):
                copy.start()

        use(pl.ds(pl.multiple_of(i * size, 8), size), *sums)
        return 0

    lax.fori_loop(0, pieces, piece, 0)


def stream_scratch(hidden, rows, wide):
    size = rows_block(hidden, 640)
    slots = min(SLOTS, hidden // size)
    return [
        pltpu.VMEM((rows, wide), BF),
        pltpu.VMEM((slots, 2, size, wide), BF),
        pltpu.SemaphoreType.DMA((slots, 2)),
    ]


def gate_up_call(order, xa, xb, gain, gate_w, up_w, carried):
    rows, width = xa.shape
    hidden = gate_w.shape[1]
    wide = width * CORES
    first = carried is None

    def kernel(*refs):
        xa_ref, xb_ref, gain_ref, gate_ref, up_ref = refs[:5]
        if first:
            gate_out, up_out, parts_out, xg_ref, buf, sem, none_ref = refs[5:]
        else:
            gate_in, up_in, parts_in, gate_out, up_out, parts_out, xg_ref, buf, sem, _ = refs[5:]
        chip, core = place_on_line()
        chunk = chunk_at(order, chip)

        def prepare():
            parts = scaled_rows(xa_ref, xb_ref, gain_ref, xg_ref, chunk, core)
            parts_out[...] = parts if first else parts_in[...] + parts
            if first:
                none_ref[...] = jnp.zeros_like(none_ref)

        def use(at, gate, up):
            gate_out[at] = (none_ref[0:1] if first else gate_in[at]) + gate
            up_out[at] = (none_ref[0:1] if first else up_in[at]) + up

        streamed(gate_ref, up_ref, xg_ref, buf, sem, chunk, prepare, use)

    operands = [xa, xb, gain, in_hbm(gate_w), in_hbm(up_w)] + ([] if first else list(carried))
    return pl.pallas_call(
        kernel,
        in_specs=[VMEM] * 3 + [HBM] * 2 + [VMEM] * (len(operands) - 5),
        out_specs=[VMEM] * 3,
        out_shape=[
            jax.ShapeDtypeStruct((hidden, rows), F32),
            jax.ShapeDtypeStruct((hidden, rows), F32),
            jax.ShapeDtypeStruct((rows, 128), F32),
        ],
        scratch_shapes=stream_scratch(hidden, rows, wide) + [pltpu.VMEM((8, rows), F32)],
        input_output_aliases={} if first else {5: 0, 6: 1, 7: 2},
        compiler_params=pltpu.CompilerParams(vmem_limit_bytes=24 * 2**20),
        cost_estimate=cost(4 * rows * wide * hidden, 4 * wide * hidden),
        name="gate_up",
    )(*operands)


def down_copies(orders, down_ref, buf, sem):
    _, hidden, width = buf.shape
    size = rows_block(hidden, 640)
    chip, core = place_on_line()
    halves = [
        (chunk_at(order, chip) * CORES + at, order)
        for order in orders
        for at in (1 - core, core)
    ]
    return [
        [
            pltpu.make_async_copy(
                down_ref.at[
                    0, pl.ds(start, size), pl.ds(pl.multiple_of(at * width, 128), width)
                ],
                buf.at[n, pl.ds(start, size)],
                sem.at[n, start // size],
            )
            for start in range(0, hidden, size)
        ]
        for n, (at, _) in enumerate(halves)
    ]


def down_pairs(halves, h_ref, buf, none_ref, out_refs):
    width = buf.shape[2]
    cols = none_ref.shape[1]
    none_ref[...] = jnp.zeros_like(none_ref)
    for n, (copies, out_ref) in enumerate(zip(halves, out_refs)):
        for copy in copies:
            copy.wait()

        def columns(i, _):
            at = pl.ds(pl.multiple_of(i * cols, 128), cols)
            out = jnp.dot(h_ref[...], buf[n, :, at], preferred_element_type=F32)
            out_ref[:, at] = (out + none_ref[0:1]).astype(out_ref.dtype)
            return 0

        lax.fori_loop(0, width // cols, columns, 0)


def down_scratch(hidden, width, count):
    return [
        pltpu.VMEM((count, hidden, width), BF),
        pltpu.SemaphoreType.DMA((count, hidden // rows_block(hidden, 640))),
        pltpu.VMEM((8, DOWN_COLS if width % DOWN_COLS == 0 else width), F32),
    ]


def last_gate_up_call(order, down_order, xa, xb, gain, gate_w, up_w, carried, down_w):
    rows, width = xa.shape
    hidden, total = down_w.shape[1:]
    wide = width * CORES

    def kernel(*refs):
        xa_ref, xb_ref, gain_ref, gate_ref, up_ref, gate_in, up_in, parts_in, down_ref = refs[:9]
        h_ref, theirs_ref, mine_ref, xg_ref, buf, sem, ht_ref, scale_ref = refs[9:17]
        down_buf, down_sem, none_ref = refs[17:]
        chip, core = place_on_line()
        chunk = chunk_at(order, chip)

        down = down_copies([down_order], down_ref, down_buf, down_sem)

        def prepare():
            for copy in sum(down, []):
                copy.start()
            parts = scaled_rows(xa_ref, xb_ref, gain_ref, xg_ref, chunk, core) + parts_in[...]
            mean = jnp.sum(parts, axis=-1, keepdims=True) * (1.0 / total)
            scale = jnp.broadcast_to(lax.rsqrt(mean + 1e-06), (rows, 128))
            scale_ref[...] = jnp.transpose(scale)[:8]

        def use(at, gate, up):
            scale = scale_ref[0:1]
            gate = (gate_in[at] + gate) * scale
            up = (up_in[at] + up) * scale
            ht_ref[at] = gate / (1.0 + jnp.exp(-gate)) * up

        streamed(gate_ref, up_ref, xg_ref, buf, sem, chunk, prepare, use)
        h_ref[...] = jnp.transpose(ht_ref[...]).astype(BF)
        down_pairs(down, h_ref, down_buf, none_ref, (theirs_ref, mine_ref))

    return pl.pallas_call(
        kernel,
        in_specs=[VMEM] * 3 + [HBM] * 2 + [VMEM] * 3 + [HBM],
        out_specs=[VMEM] * 3,
        out_shape=[
            jax.ShapeDtypeStruct((rows, hidden), BF),
            jax.ShapeDtypeStruct((rows, width), BF),
            jax.ShapeDtypeStruct((rows, width), F32),
        ],
        scratch_shapes=stream_scratch(hidden, rows, wide)
        + [pltpu.VMEM((hidden, rows), F32), pltpu.VMEM((8, rows), F32)]
        + down_scratch(hidden, width, CORES),
        compiler_params=pltpu.CompilerParams(vmem_limit_bytes=36 * 2**20),
        cost_estimate=cost(6 * rows * wide * hidden, 6 * wide * hidden),
        name="gate_up_down",
    )(xa, xb, gain, in_hbm(gate_w), in_hbm(up_w), *carried, in_hbm(down_w))


def down_call(orders, h, down_w, width):
    rows, hidden = h.shape
    count = CORES * len(orders)

    def kernel(h_ref, down_ref, *refs):
        buf, sem, none_ref = refs[count:]
        halves = down_copies(orders, down_ref, buf, sem)
        for copy in sum(halves, []):
            copy.start()
        down_pairs(halves, h_ref, buf, none_ref, refs[:count])

    return pl.pallas_call(
        kernel,
        in_specs=[VMEM, HBM],
        out_specs=[VMEM] * count,
        out_shape=[jax.ShapeDtypeStruct((rows, width), (BF, F32)[n % 2]) for n in range(count)],
        scratch_shapes=down_scratch(hidden, width, count),
        compiler_params=pltpu.CompilerParams(vmem_limit_bytes=12 * len(orders) * 2**20),
        cost_estimate=cost(4 * rows * width * hidden, 4 * width * hidden),
        name="down",
    )(h, in_hbm(down_w))


def audio_rows(enc_states, ln_gain, ln_bias):
    local_clips, frame_len, enc_width = enc_states.shape
    clip_rows = frame_len // 2
    pairs = enc_states.astype(F32).reshape(local_clips, clip_rows, 2, enc_width)
    pooled = 0.5 * (pairs[:, :, 0] + pairs[:, :, 1])
    centre = jnp.mean(pooled, axis=-1, keepdims=True)
    centred = pooled - centre
    spread = jnp.mean(centred * centred, axis=-1, keepdims=True)
    audio_ln = (centred * lax.rsqrt(spread + 1e-05) * ln_gain + ln_bias).astype(BF)
    return audio_ln.reshape(local_clips * clip_rows, enc_width)


def embedded_rows(gathered, clip_rows, clip_frames, clip_offset, w_proj, proj_bias, text_embed):
    tokens, micro, feat_local = text_embed.shape
    slots = tokens * micro
    summed = jnp.dot(gathered, w_proj, preferred_element_type=F32)
    projected = (summed + proj_bias).astype(BF)
    within = jnp.arange(clip_rows, dtype=jnp.int32)
    live = within[None, :] * 2 < clip_frames[:, None]
    spot = clip_offset[:, None] + within[None, :]
    target = jnp.where(live, spot % tokens * micro + spot // tokens, slots).reshape(-1)
    match = jnp.arange(slots, dtype=jnp.int32)[:, None] == target[None, :]
    placed = jnp.dot(match.astype(BF), projected, preferred_element_type=F32).astype(BF)
    flags = jnp.any(match, axis=1, keepdims=True)
    return jnp.where(flags, placed, text_embed.reshape(slots, feat_local))


def line_program(
    enc_states, clip_frames, clip_offset, ln_gain, ln_bias, w_proj, proj_bias, text_embed,
    norm_gain, w_gate, w_up, w_down,
):
    sections, parts = lax.axis_size("section"), lax.axis_size("fsdp")
    chips = parts // CORES
    both = ("section", "fsdp")
    section, part = lax.axis_index("section"), lax.axis_index("fsdp")
    tokens, micro, width = text_embed.shape
    rows = tokens * micro

    def exchange(value, order=0, over=0, other_core=0):
        bits = (over * chips + order) * CORES + other_core
        return lax.ppermute(value, both, [(at, at ^ bits) for at in range(sections * parts)])

    def swap(value):
        return exchange(value, other_core=1)

    rows_here = audio_rows(enc_states, ln_gain, ln_bias)
    beside = lax.ppermute(rows_here, "fsdp", [(i, i ^ 1) for i in range(parts)])
    chip_rows = jnp.concatenate([rows_here, beside], axis=0)
    gathered = [chip_rows]
    for shift in range(1, chips):
        hop = [(i, i ^ (shift * CORES)) for i in range(parts)]
        gathered.append(lax.ppermute(chip_rows, "fsdp", hop))
    position = jnp.arange(parts, dtype=jnp.int32)
    source = part ^ position
    pick = source[:, None] == position[None, :]

    def in_order(per_clip):
        local = per_clip.reshape(parts, -1)
        return jnp.sum(jnp.where(pick[:, :, None], local[None], 0), axis=1).reshape(-1)

    clip_rows = enc_states.shape[1] // 2
    stream = embedded_rows(
        jnp.concatenate(gathered, axis=0), clip_rows, in_order(clip_frames),
        in_order(clip_offset), w_proj, proj_bias, text_embed,
    )
    for stage in range(sections):
        onward = stage ^ (stage + 1) if stage + 1 < sections else 0
        taken = {0: stream, 1: exchange(stream, 1)}
        taken[3] = exchange(stream, 3)
        taken[2] = exchange(taken[3], 1)
        carried = None
        for order in (0, 1, 3):
            other = swap(taken[order])
            carried = gate_up_call(order, taken[order], other, norm_gain, w_gate, w_up, carried)
        other = swap(taken[2])
        h, theirs, mine = last_gate_up_call(
            2, 2, taken[2], other, norm_gain, w_gate, w_up, carried, w_down
        )
        across = mine + swap(theirs).astype(F32)
        across = exchange(across.astype(BF), 1).astype(F32)
        sums = down_call([1, 3], h, w_down, width)
        pair, mirrored = [
            mine + swap(theirs).astype(F32) for theirs, mine in zip(sums[::2], sums[1::2])
        ]
        pair = exchange(pair.astype(BF), 1).astype(F32)
        mirrored = exchange((mirrored + across).astype(BF), 3, onward).astype(F32)
        theirs, mine = down_call([0], h, w_down, width)
        own = mine + swap(theirs).astype(F32)
        own = own + stream.astype(F32) + pair
        if onward:
            own = exchange(own.astype(BF), 0, onward).astype(F32)
        stream = (own + mirrored).astype(BF)
    out_rows = rows // sections
    final = 0.0
    for target in range(sections):
        block = stream[target * out_rows : (target + 1) * out_rows]
        if target == sections - 1:
            kept = block
        else:
            kept = exchange(block, over=target ^ (sections - 1))
        final = final + jnp.where(section == target, kept, 0).astype(F32)
    return final.astype(BF).reshape(tokens // sections, micro, width)


def general_program(
    enc_states, clip_frames, clip_offset, ln_gain, ln_bias, w_proj, proj_bias, text_embed,
    norm_gain, w_gate, w_up, w_down,
):
    sections = lax.axis_size("section")
    section = lax.axis_index("section")
    tokens, micro, width = text_embed.shape
    rows = tokens * micro
    gathered = lax.all_gather(
        audio_rows(enc_states, ln_gain, ln_bias), "fsdp", axis=0, tiled=True
    )
    clip_rows = enc_states.shape[1] // 2
    stream = embedded_rows(
        gathered, clip_rows, clip_frames, clip_offset, w_proj, proj_bias, text_embed
    )
    gate_w, up_w, down_w = w_gate[0], w_up[0], w_down[0]
    for stage in range(sections):
        whole = lax.all_gather(stream, "fsdp", axis=1, tiled=True)
        values = whole.astype(F32)
        scale = lax.rsqrt(jnp.mean(values * values, axis=-1, keepdims=True) + 1e-06)
        normed = (values * scale * norm_gain).astype(BF)
        gate = lax.dot_general(normed, gate_w, ROWS_BOTH, preferred_element_type=F32)
        up = lax.dot_general(normed, up_w, ROWS_BOTH, preferred_element_type=F32)
        hidden = (jax.nn.silu(gate) * up).astype(BF)
        summed = jnp.dot(hidden, down_w, preferred_element_type=F32)
        branch = lax.psum_scatter(summed, "fsdp", scatter_dimension=1, tiled=True)
        stream = (stream.astype(F32) + branch).astype(BF)
        if stage + 1 < sections:
            stream = lax.ppermute(stream, "section", [(stage, stage + 1)])
    out_rows = rows // sections
    out = 0.0
    for target in range(sections):
        block = stream[target * out_rows : (target + 1) * out_rows]
        if target == sections - 1:
            out = out + jnp.where(section == target, block, 0).astype(F32)
        else:
            out = out + lax.ppermute(block, "section", [(sections - 1, target)]).astype(F32)
    return out.astype(BF).reshape(tokens // sections, micro, width)


def solution(mesh):
    placed = (
        P("fsdp", None, None),
        P(),
        P(),
        P(),
        P(),
        P(None, "fsdp"),
        P("fsdp"),
        P(None, None, "fsdp"),
        P("section", None),
        P("section", "fsdp", None),
        P("section", "fsdp", None),
        P("section", "fsdp", None),
    )
    chips = mesh.shape["fsdp"] // CORES
    sections = mesh.shape["section"]
    line = chips == LINE_CHIPS and sections & (sections - 1) == 0
    return jax.shard_map(
        line_program if line else general_program,
        mesh=mesh,
        in_specs=placed,
        out_specs=P("section", None, "fsdp"),
        check_vma=False,
    )
```

```python
import jax
import jax.numpy as jnp
from jax import lax
from jax.experimental import pallas as pl
from jax.experimental.pallas import tpu as pltpu
from jax.sharding import PartitionSpec as P


BF = jnp.bfloat16
F32 = jnp.float32
ROWS_BOTH = (((1,), (1,)), ((), ()))
CORES = 2
LINE_CHIPS = 4


def rows_block(total, most):
    best = total
    for size in range(8, min(total, most) + 1, 8):
        if total % size == 0:
            best = size
    return best


def cost(flops, nbytes):
    return pl.CostEstimate(flops=flops, bytes_accessed=nbytes, transcendentals=0)


VMEM = pl.BlockSpec(memory_space=pltpu.VMEM)
HBM = pl.BlockSpec(memory_space=pltpu.HBM)


def place_on_line():
    part = lax.axis_index("fsdp")
    return part // CORES, part % CORES


def chunk_at(order, chip):
    return chip ^ order


def scaled_rows(xa_ref, xb_ref, gain_ref, xg_ref, chunk, core):
    width = xa_ref.shape[1]
    parts = 0.0
    for x_ref, at in ((xa_ref, core), (xb_ref, 1 - core)):
        values = x_ref[...].astype(F32)
        squares = values * values
        for start in range(0, width, 128):
            parts = parts + squares[:, start : start + 128]
        gain = gain_ref[:, pl.ds(pl.multiple_of((chunk * CORES + at) * width, 128), width)]
        xg_ref[:, pl.ds(pl.multiple_of(at * width, 128), width)] = (values * gain).astype(BF)
    return parts


def in_hbm(w):
    return pltpu.with_memory_space_constraint(w, pltpu.HBM)


SLOTS = 3
DOWN_COLS = 256


def streamed(gate_ref, up_ref, xg_ref, buf, sem, chunk, prepare, use, each=None):
    slots, _, size, wide = buf.shape
    pieces = gate_ref.shape[1] // size
    start = pl.multiple_of(chunk * wide, 128)

    def copies(i):
        return [
            pltpu.make_async_copy(
                w_ref.at[0, pl.ds(pl.multiple_of(i * size, 8), size), pl.ds(start, wide)],
                buf.at[i % slots, n],
                sem.at[i % slots, n],
            )
            for n, w_ref in enumerate((gate_ref, up_ref))
        ]

    for i in range(slots):
        for copy in copies(i):
            copy.start()
    prepare()

    def single(i, n):
        pltpu.make_async_copy(
            gate_ref.at[0, pl.ds(0, size), pl.ds(start, wide)], buf.at[i % slots, n], sem.at[i % slots, n]
        ).wait()
        sums = lax.dot_general(buf[i % slots, n], xg_ref[...], ROWS_BOTH, preferred_element_type=F32)
        each(n, pl.ds(pl.multiple_of(i * size, 8), size), sums)

    def alone(k, _):
        single(k // 2, k % 2)
        return 0

    if each is not None and slots == pieces:
        lax.fori_loop(0, 2 * pieces, alone, 0)
        return

    def piece(i, _):
        sums = []
        for n, copy in enumerate(copies(i)):
            copy.wait()
            sums.append(
                lax.dot_general(
                    buf[i % slots, n], xg_ref[...], ROWS_BOTH, preferred_element_type=F32
                )
            )

        @pl.when(i + slots < pieces)
        def _():
            for copy in copies(i + slots):
                copy.start()

        use(pl.ds(pl.multiple_of(i * size, 8), size), *sums)
        return 0

    lax.fori_loop(0, pieces, piece, 0)


def stream_scratch(hidden, rows, wide):
    size = rows_block(hidden, 640)
    slots = min(SLOTS, hidden // size)
    return [
        pltpu.VMEM((rows, wide), BF),
        pltpu.VMEM((slots, 2, size, wide), BF),
        pltpu.SemaphoreType.DMA((slots, 2)),
    ]


def gate_up_call(order, xa, xb, gain, gate_w, up_w, carried):
    rows, width = xa.shape
    hidden = gate_w.shape[1]
    wide = width * CORES
    first = carried is None

    def kernel(*refs):
        xa_ref, xb_ref, gain_ref, gate_ref, up_ref = refs[:5]
        if first:
            sums_out, parts_out, xg_ref, buf, sem, none_ref = refs[5:]
        else:
            sums_in, parts_in, sums_out, parts_out, xg_ref, buf, sem, _ = refs[5:]
        chip, core = place_on_line()
        chunk = chunk_at(order, chip)

        def prepare():
            parts = scaled_rows(xa_ref, xb_ref, gain_ref, xg_ref, chunk, core)
            parts_out[...] = parts if first else parts_in[...] + parts
            if first:
                none_ref[...] = jnp.zeros_like(none_ref)

        def each(n, at, sums):
            sums_out[n, at] = (none_ref[0:1] if first else sums_in[n, at]) + sums

        def use(at, gate, up):
            each(0, at, gate)
            each(1, at, up)

        streamed(gate_ref, up_ref, xg_ref, buf, sem, chunk, prepare, use, each)

    operands = [xa, xb, gain, in_hbm(gate_w), in_hbm(up_w)] + ([] if first else list(carried))
    return pl.pallas_call(
        kernel,
        in_specs=[VMEM] * 3 + [HBM] * 2 + [VMEM] * (len(operands) - 5),
        out_specs=[VMEM] * 2,
        out_shape=[
            jax.ShapeDtypeStruct((2, hidden, rows), F32),
            jax.ShapeDtypeStruct((rows, 128), F32),
        ],
        scratch_shapes=stream_scratch(hidden, rows, wide) + [pltpu.VMEM((8, rows), F32)],
        input_output_aliases={} if first else {5: 0, 6: 1},
        compiler_params=pltpu.CompilerParams(vmem_limit_bytes=24 * 2**20),
        cost_estimate=cost(4 * rows * wide * hidden, 4 * wide * hidden),
        name="gate_up",
    )(*operands)


def down_copies(orders, down_ref, buf, sem):
    _, hidden, width = buf.shape
    size = rows_block(hidden, 640)
    chip, core = place_on_line()
    halves = [
        (chunk_at(order, chip) * CORES + at, order)
        for order in orders
        for at in (1 - core, core)
    ]
    return [
        [
            pltpu.make_async_copy(
                down_ref.at[
                    0, pl.ds(start, size), pl.ds(pl.multiple_of(at * width, 128), width)
                ],
                buf.at[n, pl.ds(start, size)],
                sem.at[n, start // size],
            )
            for start in range(0, hidden, size)
        ]
        for n, (at, _) in enumerate(halves)
    ]


def down_pairs(halves, h_ref, buf, none_ref, out_refs):
    width = buf.shape[2]
    cols = none_ref.shape[1]
    none_ref[...] = jnp.zeros_like(none_ref)
    for n, (copies, out_ref) in enumerate(zip(halves, out_refs)):
        for copy in copies:
            copy.wait()

        def columns(i, _):
            at = pl.ds(pl.multiple_of(i * cols, 128), cols)
            out = jnp.dot(h_ref[...], buf[n, :, at], preferred_element_type=F32)
            out_ref[:, at] = (out + none_ref[0:1]).astype(out_ref.dtype)
            return 0

        lax.fori_loop(0, width // cols, columns, 0)


def down_scratch(hidden, width, count):
    return [
        pltpu.VMEM((count, hidden, width), BF),
        pltpu.SemaphoreType.DMA((count, hidden // rows_block(hidden, 640))),
        pltpu.VMEM((8, DOWN_COLS if width % DOWN_COLS == 0 else width), F32),
    ]


def last_gate_up_call(order, down_order, xa, xb, gain, gate_w, up_w, carried, down_w):
    rows, width = xa.shape
    hidden, total = down_w.shape[1:]
    wide = width * CORES

    def kernel(*refs):
        xa_ref, xb_ref, gain_ref, gate_ref, up_ref, sums_in, parts_in, down_ref = refs[:8]
        h_ref, theirs_ref, mine_ref, xg_ref, buf, sem, ht_ref, scale_ref = refs[8:16]
        down_buf, down_sem, none_ref = refs[16:]
        chip, core = place_on_line()
        chunk = chunk_at(order, chip)

        down = down_copies([down_order], down_ref, down_buf, down_sem)

        def prepare():
            for copy in sum(down, []):
                copy.start()
            parts = scaled_rows(xa_ref, xb_ref, gain_ref, xg_ref, chunk, core) + parts_in[...]
            mean = jnp.sum(parts, axis=-1, keepdims=True) * (1.0 / total)
            scale = jnp.broadcast_to(lax.rsqrt(mean + 1e-06), (rows, 128))
            scale_ref[...] = jnp.transpose(scale)[:8]

        def use(at, gate, up):
            scale = scale_ref[0:1]
            gate = (sums_in[0, at] + gate) * scale
            up = (sums_in[1, at] + up) * scale
            ht_ref[at] = gate / (1.0 + jnp.exp(-gate)) * up

        streamed(gate_ref, up_ref, xg_ref, buf, sem, chunk, prepare, use)
        h_ref[...] = jnp.transpose(ht_ref[...]).astype(BF)
        down_pairs(down, h_ref, down_buf, none_ref, (theirs_ref, mine_ref))

    return pl.pallas_call(
        kernel,
        in_specs=[VMEM] * 3 + [HBM] * 2 + [VMEM] * 2 + [HBM],
        out_specs=[VMEM] * 3,
        out_shape=[
            jax.ShapeDtypeStruct((rows, hidden), BF),
            jax.ShapeDtypeStruct((rows, width), BF),
            jax.ShapeDtypeStruct((rows, width), F32),
        ],
        scratch_shapes=stream_scratch(hidden, rows, wide)
        + [pltpu.VMEM((hidden, rows), F32), pltpu.VMEM((8, rows), F32)]
        + down_scratch(hidden, width, CORES),
        compiler_params=pltpu.CompilerParams(vmem_limit_bytes=36 * 2**20),
        cost_estimate=cost(6 * rows * wide * hidden, 6 * wide * hidden),
        name="gate_up_down",
    )(xa, xb, gain, in_hbm(gate_w), in_hbm(up_w), *carried, in_hbm(down_w))


def down_call(orders, h, down_w, width):
    rows, hidden = h.shape
    count = CORES * len(orders)

    def kernel(h_ref, down_ref, *refs):
        buf, sem, none_ref = refs[count:]
        halves = down_copies(orders, down_ref, buf, sem)
        for copy in sum(halves, []):
            copy.start()
        down_pairs(halves, h_ref, buf, none_ref, refs[:count])

    return pl.pallas_call(
        kernel,
        in_specs=[VMEM, HBM],
        out_specs=[VMEM] * count,
        out_shape=[jax.ShapeDtypeStruct((rows, width), (BF, F32)[n % 2]) for n in range(count)],
        scratch_shapes=down_scratch(hidden, width, count),
        compiler_params=pltpu.CompilerParams(vmem_limit_bytes=12 * len(orders) * 2**20),
        cost_estimate=cost(4 * rows * width * hidden, 4 * width * hidden),
        name="down",
    )(h, in_hbm(down_w))


def audio_rows(enc_states, ln_gain, ln_bias):
    local_clips, frame_len, enc_width = enc_states.shape
    clip_rows = frame_len // 2
    pairs = enc_states.astype(F32).reshape(local_clips, clip_rows, 2, enc_width)
    pooled = 0.5 * (pairs[:, :, 0] + pairs[:, :, 1])
    centre = jnp.mean(pooled, axis=-1, keepdims=True)
    centred = pooled - centre
    spread = jnp.mean(centred * centred, axis=-1, keepdims=True)
    audio_ln = (centred * lax.rsqrt(spread + 1e-05) * ln_gain + ln_bias).astype(BF)
    return audio_ln.reshape(local_clips * clip_rows, enc_width)


def embedded_rows(gathered, clip_rows, clip_frames, clip_offset, w_proj, proj_bias, text_embed):
    tokens, micro, feat_local = text_embed.shape
    slots = tokens * micro
    summed = jnp.dot(gathered, w_proj, preferred_element_type=F32)
    projected = (summed + proj_bias).astype(BF)
    within = jnp.arange(clip_rows, dtype=jnp.int32)
    live = within[None, :] * 2 < clip_frames[:, None]
    spot = clip_offset[:, None] + within[None, :]
    target = jnp.where(live, spot % tokens * micro + spot // tokens, slots).reshape(-1)
    match = jnp.arange(slots, dtype=jnp.int32)[:, None] == target[None, :]
    placed = jnp.dot(match.astype(BF), projected, preferred_element_type=F32).astype(BF)
    flags = jnp.any(match, axis=1, keepdims=True)
    return jnp.where(flags, placed, text_embed.reshape(slots, feat_local))


def line_program(
    enc_states, clip_frames, clip_offset, ln_gain, ln_bias, w_proj, proj_bias, text_embed,
    norm_gain, w_gate, w_up, w_down,
):
    sections, parts = lax.axis_size("section"), lax.axis_size("fsdp")
    chips = parts // CORES
    both = ("section", "fsdp")
    section, part = lax.axis_index("section"), lax.axis_index("fsdp")
    tokens, micro, width = text_embed.shape
    rows = tokens * micro

    def exchange(value, order=0, over=0, other_core=0):
        bits = (over * chips + order) * CORES + other_core
        return lax.ppermute(value, both, [(at, at ^ bits) for at in range(sections * parts)])

    def swap(value):
        return exchange(value, other_core=1)

    rows_here = audio_rows(enc_states, ln_gain, ln_bias)
    beside = lax.ppermute(rows_here, "fsdp", [(i, i ^ 1) for i in range(parts)])
    chip_rows = jnp.concatenate([rows_here, beside], axis=0)
    gathered = [chip_rows]
    for shift in range(1, chips):
        hop = [(i, i ^ (shift * CORES)) for i in range(parts)]
        gathered.append(lax.ppermute(chip_rows, "fsdp", hop))
    position = jnp.arange(parts, dtype=jnp.int32)
    source = part ^ position
    pick = source[:, None] == position[None, :]

    def in_order(per_clip):
        local = per_clip.reshape(parts, -1)
        return jnp.sum(jnp.where(pick[:, :, None], local[None], 0), axis=1).reshape(-1)

    clip_rows = enc_states.shape[1] // 2
    stream = embedded_rows(
        jnp.concatenate(gathered, axis=0), clip_rows, in_order(clip_frames),
        in_order(clip_offset), w_proj, proj_bias, text_embed,
    )
    for stage in range(sections):
        onward = stage ^ (stage + 1) if stage + 1 < sections else 0
        taken = {0: stream, 1: exchange(stream, 1)}
        taken[3] = exchange(stream, 3)
        taken[2] = exchange(taken[3], 1)
        carried = None
        for order in (0, 1, 3):
            other = swap(taken[order])
            carried = gate_up_call(order, taken[order], other, norm_gain, w_gate, w_up, carried)
        other = swap(taken[2])
        h, theirs, mine = last_gate_up_call(
            2, 2, taken[2], other, norm_gain, w_gate, w_up, carried, w_down
        )
        across = mine + swap(theirs).astype(F32)
        across = exchange(across.astype(BF), 1).astype(F32)
        sums = down_call([1, 3], h, w_down, width)
        pair, mirrored = [
            mine + swap(theirs).astype(F32) for theirs, mine in zip(sums[::2], sums[1::2])
        ]
        pair = exchange(pair.astype(BF), 1).astype(F32)
        mirrored = exchange((mirrored + across).astype(BF), 3, onward).astype(F32)
        theirs, mine = down_call([0], h, w_down, width)
        own = mine + swap(theirs).astype(F32)
        own = own + stream.astype(F32) + pair
        if onward:
            own = exchange(own.astype(BF), 0, onward).astype(F32)
        stream = (own + mirrored).astype(BF)
    out_rows = rows // sections
    final = 0.0
    for target in range(sections):
        block = stream[target * out_rows : (target + 1) * out_rows]
        if target == sections - 1:
            kept = block
        else:
            kept = exchange(block, over=target ^ (sections - 1))
        final = final + jnp.where(section == target, kept, 0).astype(F32)
    return final.astype(BF).reshape(tokens // sections, micro, width)


def general_program(
    enc_states, clip_frames, clip_offset, ln_gain, ln_bias, w_proj, proj_bias, text_embed,
    norm_gain, w_gate, w_up, w_down,
):
    sections = lax.axis_size("section")
    section = lax.axis_index("section")
    tokens, micro, width = text_embed.shape
    rows = tokens * micro
    gathered = lax.all_gather(
        audio_rows(enc_states, ln_gain, ln_bias), "fsdp", axis=0, tiled=True
    )
    clip_rows = enc_states.shape[1] // 2
    stream = embedded_rows(
        gathered, clip_rows, clip_frames, clip_offset, w_proj, proj_bias, text_embed
    )
    gate_w, up_w, down_w = w_gate[0], w_up[0], w_down[0]
    for stage in range(sections):
        whole = lax.all_gather(stream, "fsdp", axis=1, tiled=True)
        values = whole.astype(F32)
        scale = lax.rsqrt(jnp.mean(values * values, axis=-1, keepdims=True) + 1e-06)
        normed = (values * scale * norm_gain).astype(BF)
        gate = lax.dot_general(normed, gate_w, ROWS_BOTH, preferred_element_type=F32)
        up = lax.dot_general(normed, up_w, ROWS_BOTH, preferred_element_type=F32)
        hidden = (jax.nn.silu(gate) * up).astype(BF)
        summed = jnp.dot(hidden, down_w, preferred_element_type=F32)
        branch = lax.psum_scatter(summed, "fsdp", scatter_dimension=1, tiled=True)
        stream = (stream.astype(F32) + branch).astype(BF)
        if stage + 1 < sections:
            stream = lax.ppermute(stream, "section", [(stage, stage + 1)])
    out_rows = rows // sections
    out = 0.0
    for target in range(sections):
        block = stream[target * out_rows : (target + 1) * out_rows]
        if target == sections - 1:
            out = out + jnp.where(section == target, block, 0).astype(F32)
        else:
            out = out + lax.ppermute(block, "section", [(sections - 1, target)]).astype(F32)
    return out.astype(BF).reshape(tokens // sections, micro, width)


def solution(mesh):
    placed = (
        P("fsdp", None, None),
        P(),
        P(),
        P(),
        P(),
        P(None, "fsdp"),
        P("fsdp"),
        P(None, None, "fsdp"),
        P("section", None),
        P("section", "fsdp", None),
        P("section", "fsdp", None),
        P("section", "fsdp", None),
    )
    chips = mesh.shape["fsdp"] // CORES
    sections = mesh.shape["section"]
    line = chips == LINE_CHIPS and sections & (sections - 1) == 0
    return jax.shard_map(
        line_program if line else general_program,
        mesh=mesh,
        in_specs=placed,
        out_specs=P("section", None, "fsdp"),
        check_vma=False,
    )
```
